32 devices in a mesh: facet: 4 (over z), pol: 4 (over y, x), tm: 2 (over core).
Axes of the slice: x: 2, y: 2, z: 4, core: 2. Of those that a mesh axis runs over, the one named last changes fastest.
Arguments:
- tile_spectral_lines: bfloat16 [64, 4, 2, 64, 4096], P('facet', 'pol', None, 'tm'), may hold values from -6 to 6
- taper_leading_axis: bfloat16 [4, 2, 128, 512], P('facet', 'tm'), may hold values from -0.25 to 0.25
- taper_trailing_axis: bfloat16 [4, 2, 128, 512], P('facet', 'tm'), may hold values from -0.25 to 0.25
- depth_layer_factors: bfloat16 [4, 2, 2, 128], P('facet', 'tm'), may hold values from -4 to 4
- measured_correlations: float32 [4, 8, 2, 128], P('facet', None, 'tm', 'pol'), may hold values from -6 to 6
- visibility_groups_table: int32 [4, 2, 3, 8], P('facet', 'tm'), may hold values from 0 to 130815, as said below
- antenna_links: int32 [2, 130816], replicated, may hold values from 0 to 511, as said below
- complex_receiver_factors: float32 [256, 4, 512], replicated, may hold values from -5 to 5
Outputs:
- residual: float32 [4, 8, 2, 128], P('facet', None, 'tm', 'pol')
- gain_grad: float32 [512, 1024], P(('facet', 'pol', 'tm'))
The draws below stay inside these ranges and needn't reach their ends.
Inputs may be any that keep to these rules, and one draw needn't show every extreme that they name: `visibility_groups_table`: for each subgrid and owner, every block has a channel below 256, a count of 1 or more, and baselines offset to offset + count - 1 below 130816; the counts of one owner sum to at most 128, and some owner reaches 128 in every draw. `antenna_links`: each baseline joins two different stations.
All inputs are finite; a program needn't handle non-finite values.
Results may differ from the reference program's by a relative error of at most 0.012.
Values may be sent and summed in bfloat16 or wider, within the bound.
A program may use at most 192 MiB of HBM per device.

```python
import math
import jax
import jax.numpy as jnp
import numpy as np
from jax import lax

FGRID = 8
NF = 64
FS = 4096
MC = 64
SG = 512
NPOL = 4
NW = 2
NSUB = 4
TMO = 2
VT = 128
NBLK = 8
NCH = 256
NST = 512
NBASE = 130816


def draw_visibility_groups_table(key, part):
    subkeys = jax.random.split(jax.random.fold_in(key, 4101), 5)
    owners_all = NSUB * TMO
    raw_draw = jax.random.randint(subkeys[0], (owners_all,), 0, VT + 1)
    base_load = VT // 16
    owner_loads = base_load + raw_draw * raw_draw * (VT - base_load) // (VT * VT)
    chosen = jax.random.randint(subkeys[1], (), 0, owners_all)
    owner_loads = jnp.where(jnp.arange(owners_all) == chosen, VT, owner_loads)
    weights = jax.random.randint(subkeys[2], (owners_all, NBLK), 1, 17)
    spare_load = owner_loads - NBLK
    amounts = 1 + spare_load[:, None] * weights // jnp.sum(weights, axis=1, keepdims=True)
    amounts = amounts.at[:, NBLK - 1].set(owner_loads - jnp.sum(amounts[:, :NBLK - 1], axis=1))
    channels = jax.random.randint(subkeys[3], (owners_all, NBLK), 0, NCH)
    offsets = jax.random.randint(subkeys[4], (owners_all, NBLK), 0, NBASE - VT + 1)
    block_table = jnp.stack([channels, offsets, amounts], axis=1)
    return block_table.reshape(NSUB, TMO, 3, NBLK).astype(jnp.int32)


def draw_antenna_links(key, part):
    subkeys = jax.random.split(jax.random.fold_in(key, 7723), 2)
    antenna_left = jax.random.randint(subkeys[0], (NBASE,), 0, NST)
    step_ahead = jax.random.randint(subkeys[1], (NBASE,), 1, NST)
    antenna_right = (antenna_left + step_ahead) % NST
    return jnp.stack([antenna_left, antenna_right]).astype(jnp.int32)


def levels(key, dims, cuts, low, high):
    factor_of, own = 1.0, jax.random.fold_in(key, 6)
    for dim, blocks in cuts:
        steps = jnp.exp(jax.random.uniform(jax.random.fold_in(own, dim), (blocks,), jnp.float32, low / len(cuts), high / len(cuts)))
        factor_of = factor_of * jnp.repeat(steps, dims[dim] // blocks).reshape([-1 if axis == dim else 1 for axis in range(len(dims))])
    return factor_of


def noise(own_key, extent, width, bound, cuts=(), held_as=jnp.bfloat16):
    gain = levels(own_key, extent, cuts, -0.22, 0.18) if cuts else 1.0
    drawn = jax.random.normal(own_key, extent, jnp.float32) * width * gain
    return jnp.minimum(jnp.maximum(drawn, -bound), bound).astype(held_as)


def setup_inputs(seed: int = 0) -> dict:
    keys = jax.random.split(jax.random.key(seed), 9)
    tile_spectral_lines = noise(keys[0], (NF, NPOL, 2, MC, FS), 1.0, 6.0, ((0, 4), (1, 4), (3, 2)))
    taper_leading_axis = noise(keys[1], (NSUB, TMO, VT, SG), SG ** -0.5, 0.25, ((0, 4), (1, 2)))
    taper_trailing_axis = noise(keys[2], (NSUB, TMO, VT, SG), SG ** -0.5, 0.25, ((0, 4), (1, 2)))
    depth_layer_factors = noise(keys[3], (NSUB, TMO, NW, VT), NW ** -0.5, 4.0, ((0, 4), (1, 2)))
    measured_correlations = noise(keys[4], (NSUB, 2 * NPOL, TMO, VT), 1.0, 6.0, ((0, 4), (2, 2), (3, 4)), jnp.float32)
    visibility_groups_table = draw_visibility_groups_table(jax.random.fold_in(keys[8], 71), 0)
    antenna_links = draw_antenna_links(jax.random.fold_in(keys[8], 71), 0)
    complex_receiver_factors = noise(keys[7], (NCH, 4, NST), 0.8, 5.0, (), jnp.float32)
    return dict(tile_spectral_lines=tile_spectral_lines, taper_leading_axis=taper_leading_axis, taper_trailing_axis=taper_trailing_axis, depth_layer_factors=depth_layer_factors, measured_correlations=measured_correlations, visibility_groups_table=visibility_groups_table, antenna_links=antenna_links, complex_receiver_factors=complex_receiver_factors)


w_chirp = 0.37
grad_scale = 0.1
feed_first = np.array([0, 0, 1, 1])
feed_second = np.array([0, 1, 0, 1])

def dft_table(length):
    indices = jnp.arange(length, dtype=jnp.int32)
    product = indices[:, None] * indices[None, :] % length
    angles = 2.0 * math.pi / length * product.astype(jnp.float32)
    factor = 1.0 / math.sqrt(length)
    return ((jnp.cos(angles) * factor).astype(jnp.bfloat16), (jnp.sin(angles) * factor).astype(jnp.bfloat16))

def chirp_phase(first_row, row_total, side_cells):
    across = (first_row + jnp.arange(row_total, dtype=jnp.int32) - side_cells // 2).astype(jnp.float32)
    downward = (jnp.arange(side_cells, dtype=jnp.int32) - side_cells // 2).astype(jnp.float32)
    return w_chirp * (across[:, None] * across[:, None] + downward[None, :] * downward[None, :]) / float(side_cells * side_cells)

def make_planes(sub_real, sub_imag, phase_grid, layers):
    planes_list = []
    for plane_index in range(layers):
        angles = 2.0 * math.pi * plane_index * phase_grid
        cosine = jnp.cos(angles)
        sine_part = jnp.sin(angles)
        planes_list.append(jnp.stack([sub_real * cosine - sub_imag * sine_part, sub_real * sine_part + sub_imag * cosine]).astype(jnp.bfloat16))
    return jnp.stack(planes_list)

def decode_slots(block_table, slot_index):
    channels = block_table[..., 0, :]
    offsets = block_table[..., 1, :]
    amounts = block_table[..., 2, :]
    starts = (jnp.cumsum(amounts, axis=-1) - amounts).astype(jnp.int32)
    relative = (slot_index[:, None] - starts[..., None, :]).astype(jnp.int32)
    member = ((relative >= 0) & (relative < amounts[..., None, :])).astype(jnp.int32)
    slot_live = lax.optimization_barrier(jnp.sum(member, axis=-1)).astype(jnp.int32)
    channel = lax.optimization_barrier(jnp.sum(member * channels[..., None, :], axis=-1)).astype(jnp.int32)
    antenna_couple = lax.optimization_barrier(jnp.sum(member * (offsets[..., None, :] + relative), axis=-1)).astype(jnp.int32)
    return (slot_live, channel, antenna_couple)

def model_terms(pred_re, pred_im, obs_re, obs_im, gain_first, gain_second, slot_live):
    first_re = gain_first[..., 2 * feed_first]
    first_im = gain_first[..., 2 * feed_first + 1]
    second_re = gain_second[..., 2 * feed_second]
    second_im = gain_second[..., 2 * feed_second + 1]
    both_re = first_re * second_re + first_im * second_im
    both_im = first_im * second_re - first_re * second_im
    model_re = both_re * pred_re - both_im * pred_im
    model_im = both_re * pred_im + both_im * pred_re
    alive_mask = slot_live.astype(jnp.float32)[..., None]
    resid_re = alive_mask * (obs_re - model_re)
    resid_im = alive_mask * (obs_im - model_im)
    cross_re = second_re * pred_re + second_im * pred_im
    cross_im = second_im * pred_re - second_re * pred_im
    lead_re = -(resid_re * cross_re - resid_im * cross_im)
    lead_im = -(resid_re * cross_im + resid_im * cross_re)
    along_re = first_re * pred_re - first_im * pred_im
    along_im = first_re * pred_im + first_im * pred_re
    trail_re = -(resid_re * along_re + resid_im * along_im)
    trail_im = -(resid_re * along_im - resid_im * along_re)
    leading = jnp.stack([lead_re[..., 0] + lead_re[..., 1], lead_im[..., 0] + lead_im[..., 1], lead_re[..., 2] + lead_re[..., 3], lead_im[..., 2] + lead_im[..., 3]], axis=-1)
    trailing = jnp.stack([trail_re[..., 0] + trail_re[..., 2], trail_im[..., 0] + trail_im[..., 2], trail_re[..., 1] + trail_re[..., 3], trail_im[..., 1] + trail_im[..., 3]], axis=-1)
    return (resid_re, resid_im, leading, trailing)

def real_dot(left_side, right_side):
    return jnp.dot(left_side.astype(jnp.float32), right_side.astype(jnp.float32), precision=lax.Precision.HIGHEST)

def degrid_reference(layers, rows_u, rows_v, weights_w):
    spread_v = jnp.einsum('wcuv,nv->wcun', layers.astype(jnp.float32), rows_v.astype(jnp.float32), precision=lax.Precision.HIGHEST)
    along_u = lax.optimization_barrier(jnp.sum(spread_v * jnp.transpose(rows_u).astype(jnp.float32)[None, None], axis=2))
    return lax.optimization_barrier(jnp.sum(along_u * weights_w.astype(jnp.float32)[:, None, :], axis=0))

def reference(tile_spectral_lines, taper_leading_axis, taper_trailing_axis, depth_layer_factors, measured_correlations, visibility_groups_table, antenna_links, complex_receiver_factors):
    source = tile_spectral_lines.astype(jnp.float32)
    spectrum = jnp.fft.fft(source[:, :, 0] + 1j * source[:, :, 1], axis=-1)[..., :NSUB * MC] / math.sqrt(FS)
    contrib_re = jnp.real(spectrum).astype(jnp.bfloat16)
    contrib_im = jnp.imag(spectrum).astype(jnp.bfloat16)

    def assemble(pieces):
        layout = pieces.reshape(FGRID, FGRID, NPOL, MC, NSUB, MC)
        return jnp.transpose(layout, (4, 2, 0, 3, 1, 5)).reshape(NSUB, NPOL, SG, SG)
    table_re, table_im = dft_table(SG)
    phase_grid = chirp_phase(0, SG, SG)

    def one_subgrid(inputs):
        layout_re, layout_im, rows_u, rows_v, weights_w = inputs
        flat_u = rows_u.reshape(TMO * VT, SG)
        flat_v = rows_v.reshape(TMO * VT, SG)
        flat_w = jnp.transpose(weights_w, (1, 0, 2)).reshape(NW, TMO * VT)
        results = []
        for polarisation in range(NPOL):
            half_re = (real_dot(layout_re[polarisation], table_re) - real_dot(layout_im[polarisation], table_im)).astype(jnp.bfloat16)
            half_im = (real_dot(layout_re[polarisation], table_im) + real_dot(layout_im[polarisation], table_re)).astype(jnp.bfloat16)
            sub_real = (real_dot(table_re, half_re) - real_dot(table_im, half_im)).astype(jnp.bfloat16)
            sub_imag = (real_dot(table_re, half_im) + real_dot(table_im, half_re)).astype(jnp.bfloat16)
            layers = make_planes(sub_real, sub_imag, phase_grid, NW)
            results.append(degrid_reference(layers, flat_u, flat_v, flat_w))
        return jnp.stack(results).reshape(NPOL, 2, TMO, VT)
    predicted = lax.map(one_subgrid, (assemble(contrib_re), assemble(contrib_im), taper_leading_axis, taper_trailing_axis, depth_layer_factors))
    slot_index = jnp.arange(VT, dtype=jnp.int32)
    slot_live, channel, antenna_couple = decode_slots(visibility_groups_table, slot_index)
    antenna_left = jnp.take(antenna_links[0], antenna_couple)
    antenna_right = jnp.take(antenna_links[1], antenna_couple)
    gains_turned = jnp.transpose(complex_receiver_factors, (0, 2, 1))
    gain_first = gains_turned[channel, antenna_left]
    gain_second = gains_turned[channel, antenna_right]
    pred_re = jnp.transpose(predicted[:, :, 0], (0, 2, 3, 1))
    pred_im = jnp.transpose(predicted[:, :, 1], (0, 2, 3, 1))
    obs_re = jnp.transpose(measured_correlations[:, 0::2], (0, 2, 3, 1))
    obs_im = jnp.transpose(measured_correlations[:, 1::2], (0, 2, 3, 1))
    resid_re, resid_im, leading, trailing = model_terms(pred_re, pred_im, obs_re, obs_im, gain_first, gain_second, slot_live)
    residual = jnp.transpose(jnp.stack([resid_re, resid_im], axis=-1), (0, 3, 4, 1, 2)).reshape(NSUB, 2 * NPOL, TMO, VT)
    segments_first = (antenna_left * NCH + channel).reshape(-1).astype(jnp.int32)
    segments_second = (antenna_right * NCH + channel).reshape(-1).astype(jnp.int32)
    summed = jax.ops.segment_sum(leading.reshape(-1, 4), segments_first, num_segments=NST * NCH)
    summed = summed + jax.ops.segment_sum(trailing.reshape(-1, 4), segments_second, num_segments=NST * NCH)
    gain_grad = grad_scale * summed.reshape(NST, NCH * 4)
    return (residual, gain_grad)
```

```python
import functools
import math

import jax
import jax.numpy as jnp
import numpy as np
from jax import lax
from jax.experimental import pallas as pl
from jax.experimental.pallas import tpu as pltpu
from jax.sharding import PartitionSpec as P

FGRID = 8
FS = 4096
MC = 64
SG = 512
NPOL = 4
NW = 2
NCH = 256
NST = 512
CHUNK = 512

w_chirp = 0.37
grad_scale = 0.1
feed_first = np.array([0, 0, 1, 1])
feed_second = np.array([0, 1, 0, 1])


def unit_angles(left, right, length):
    product = np.outer(np.arange(left), np.arange(right)) % length
    return 2.0 * math.pi * product / length


def fourier_factors(subgrids):
    spread = FS // MC
    alpha = unit_angles(FS // spread, MC, MC)
    p = np.concatenate([np.cos(alpha), -np.sin(alpha)], axis=1) / math.sqrt(FS)
    q = np.concatenate([-np.sin(alpha), -np.cos(alpha)], axis=1) / math.sqrt(FS)
    beta = unit_angles(spread, subgrids * MC, FS).reshape(spread, subgrids, 1, MC)
    beta = np.broadcast_to(beta, (spread, subgrids, 2, MC)).reshape(spread, subgrids * 2 * MC)
    tile = lambda t: np.tile(t, (1, subgrids)).astype(np.float32)
    return (
        tile(p),
        tile(q),
        np.cos(beta).astype(np.float32),
        np.sin(beta).astype(np.float32),
    )


def fourier_kernel(p_ref, q_ref, c_ref, s_ref, x_ref, o_ref, table, total):
    step = pl.program_id(0)
    facets, _, rows, chunk = x_ref.shape
    subgrids = o_ref.shape[0]
    spread = c_ref.shape[0]
    cosine, sine = c_ref[...], s_ref[...]
    for part in range(chunk // spread):
        lead = p_ref[part : part + 1, :]
        other = q_ref[part : part + 1, :]
        table[part * spread : (part + 1) * spread, :] = (lead * cosine + other * sine).astype(
            jnp.bfloat16
        )
    x = x_ref[...].reshape(facets * 2 * rows, chunk)
    product = jnp.dot(x, table[...], preferred_element_type=jnp.float32)

    @pl.when(step == 0)
    def _():
        total[...] = product

    @pl.when(step > 0)
    def _():
        total[...] += product

    @pl.when(step == pl.num_programs(0) - 1)
    def _():
        lane = lax.broadcasted_iota(jnp.int32, (rows, 2 * MC), 1)
        sign = jnp.where(lane < MC, -1.0, 1.0)
        packed = o_ref.shape[3] // (2 * MC)
        for f in range(facets):
            for s in range(subgrids):
                cut = slice(s * 2 * MC, (s + 1) * 2 * MC)
                first = total[2 * f * rows : (2 * f + 1) * rows, cut]
                second = total[(2 * f + 1) * rows : (2 * f + 2) * rows, cut]
                value = first + sign * pltpu.roll(second, MC, 1)
                j = f % packed
                o_ref[s, f // packed, :, j * 2 * MC : (j + 1) * 2 * MC] = value.astype(jnp.bfloat16)


def fourier(x, subgrids):
    facets, _, rows, length = x.shape
    width = subgrids * 2 * MC
    spread = FS // MC
    packed = FGRID if facets % FGRID == 0 else 1
    per_step = CHUNK // spread
    factors = [jnp.asarray(t) for t in fourier_factors(subgrids)]
    return pl.pallas_call(
        fourier_kernel,
        out_shape=jax.ShapeDtypeStruct(
            (subgrids, facets // packed, rows, packed * 2 * MC), jnp.bfloat16
        ),
        grid=(length // CHUNK,),
        in_specs=[
            pl.BlockSpec((per_step, width), lambda g: (g, 0)),
            pl.BlockSpec((per_step, width), lambda g: (g, 0)),
            pl.BlockSpec((spread, width), lambda g: (0, 0)),
            pl.BlockSpec((spread, width), lambda g: (0, 0)),
            pl.BlockSpec((facets, 2, rows, CHUNK), lambda g: (0, 0, 0, g)),
        ],
        out_specs=pl.BlockSpec(
            (subgrids, facets // packed, rows, packed * 2 * MC), lambda g: (0, 0, 0, 0)
        ),
        scratch_shapes=[
            pltpu.VMEM((CHUNK, width), jnp.bfloat16),
            pltpu.VMEM((facets * 2 * rows, width), jnp.float32),
        ],
        compiler_params=pltpu.CompilerParams(
            dimension_semantics=("arbitrary",), vmem_limit_bytes=48 << 20
        ),
    )(*factors, x)


def subgrid_tables():
    angle = unit_angles(SG, SG, SG)
    re = np.cos(angle) / math.sqrt(SG)
    im = np.sin(angle) / math.sqrt(SG)
    blocks = lambda t: t.reshape(SG, FGRID, MC)
    second = np.stack([blocks(re), -blocks(im)], axis=2).reshape(SG, 2 * SG)
    third = np.stack([blocks(im), blocks(re)], axis=2).reshape(SG, 2 * SG)
    return [t.astype(jnp.bfloat16) for t in (re, im, second, third)]


def chirp_line():
    offset = np.arange(SG) - SG // 2
    angle = 2.0 * math.pi * w_chirp * (offset * offset) / float(SG * SG)
    return np.cos(angle).astype(np.float32), np.sin(angle).astype(np.float32)


def chirped(taper):
    cosine, sine = chirp_line()
    wide = taper.astype(jnp.float32)
    return jnp.concatenate(
        [taper, (wide * cosine).astype(jnp.bfloat16), (wide * sine).astype(jnp.bfloat16)], axis=0
    )


def decode_slots(block_table, slot_index):
    channels = block_table[0]
    offsets = block_table[1]
    amounts = block_table[2]
    starts = jnp.cumsum(amounts) - amounts
    relative = slot_index[:, None] - starts[None, :]
    member = ((relative >= 0) & (relative < amounts[None, :])).astype(jnp.int32)
    slot_live = jnp.sum(member, axis=-1)
    channel = jnp.sum(member * channels[None, :], axis=-1)
    baseline = jnp.sum(member * (offsets[None, :] + relative), axis=-1)
    return slot_live, channel, baseline, member


def model_terms(pred_re, pred_im, obs_re, obs_im, gain_first, gain_second, slot_live):
    first_re = gain_first[2 * feed_first]
    first_im = gain_first[2 * feed_first + 1]
    second_re = gain_second[2 * feed_second]
    second_im = gain_second[2 * feed_second + 1]
    both_re = first_re * second_re + first_im * second_im
    both_im = first_im * second_re - first_re * second_im
    model_re = both_re * pred_re - both_im * pred_im
    model_im = both_re * pred_im + both_im * pred_re
    alive_mask = slot_live.astype(jnp.float32)[None, :]
    resid_re = alive_mask * (obs_re - model_re)
    resid_im = alive_mask * (obs_im - model_im)
    cross_re = second_re * pred_re + second_im * pred_im
    cross_im = second_im * pred_re - second_re * pred_im
    lead_re = -(resid_re * cross_re - resid_im * cross_im)
    lead_im = -(resid_re * cross_im + resid_im * cross_re)
    along_re = first_re * pred_re - first_im * pred_im
    along_im = first_re * pred_im + first_im * pred_re
    trail_re = -(resid_re * along_re + resid_im * along_im)
    trail_im = -(resid_re * along_im - resid_im * along_re)
    leading = jnp.stack(
        [
            lead_re[0] + lead_re[1],
            lead_im[0] + lead_im[1],
            lead_re[2] + lead_re[3],
            lead_im[2] + lead_im[3],
        ]
    )
    trailing = jnp.stack(
        [
            trail_re[0] + trail_re[2],
            trail_im[0] + trail_im[2],
            trail_re[1] + trail_re[3],
            trail_im[1] + trail_im[3],
        ]
    )
    return resid_re, resid_im, leading, trailing


def nt_dot(left, right, **kw):
    return lax.dot_general(
        left, right, (((1,), (1,)), ((), ())), preferred_element_type=jnp.float32, **kw
    )


def on_device(
    tile_spectral_lines,
    taper_leading_axis,
    taper_trailing_axis,
    depth_layer_factors,
    measured_correlations,
    visibility_groups_table,
    antenna_links,
    complex_receiver_factors,
):
    exact = lax.Precision.HIGHEST
    subgrids = lax.axis_size("facet")
    owners = lax.axis_size("tm")
    pols = lax.axis_size("pol")
    owner_index = lax.axis_index("tm")
    slots = taper_leading_axis.shape[2]
    quarter = measured_correlations.shape[3]
    rows = tile_spectral_lines.shape[3]

    tapers = jnp.concatenate(
        [
            taper_leading_axis.reshape(slots, SG),
            taper_trailing_axis.reshape(slots, SG),
        ],
        axis=1,
    )
    partner = lax.ppermute(tapers, "tm", [(0, 1), (1, 0)])
    depth = depth_layer_factors.reshape(NW, slots)
    depth_partner = lax.ppermute(depth, "tm", [(0, 1), (1, 0)])
    both = jnp.concatenate([tapers, partner], axis=0)
    depth_both = jnp.concatenate([depth, depth_partner], axis=1).astype(jnp.float32)

    contrib = fourier(tile_spectral_lines[:, 0], subgrids)
    received = lax.all_to_all(contrib, "facet", split_axis=0, concat_axis=1, tiled=True)
    if received.shape[3] == 2 * SG:
        lines = received.reshape(FGRID * rows, 2 * SG)
    else:
        lines = jnp.transpose(
            received.reshape(FGRID, FGRID, rows, 2 * MC), (0, 2, 1, 3)
        ).reshape(FGRID * rows, 2 * SG)

    table_re, table_im, second, third = [jnp.asarray(t) for t in subgrid_tables()]
    own = 2 * slots
    trail3 = chirped(both[:, SG:])
    right_a = jnp.dot(trail3, second, preferred_element_type=jnp.float32).reshape(3, own, 2 * SG)
    right_b = jnp.dot(trail3, third, preferred_element_type=jnp.float32).reshape(3, own, 2 * SG)
    right = jnp.stack(
        [
            right_a[0],
            right_a[1] - right_b[2],
            right_b[0],
            right_b[1] + right_a[2],
        ]
    ).astype(jnp.bfloat16)
    lead3 = chirped(both[:, :SG])

    def own_rows(table):
        return lax.dynamic_index_in_dim(
            table.reshape(FGRID, owners, rows, SG), owner_index, 1, keepdims=False
        ).reshape(FGRID * rows, SG)

    left_re = nt_dot(own_rows(table_re), lead3).reshape(FGRID * rows, 3, own)
    left_im = nt_dot(own_rows(table_im), lead3).reshape(FGRID * rows, 3, own)
    lre = jnp.stack([left_re[:, 0], left_re[:, 1] - left_im[:, 2]], axis=1)
    lim = jnp.stack([left_im[:, 0], left_re[:, 2] + left_im[:, 1]], axis=1)
    spread = nt_dot(lines, right.reshape(4 * own, 2 * SG)).reshape(FGRID * rows, 2, 2, own)
    part_re = jnp.sum(jnp.sum(lre * spread[:, 0] - lim * spread[:, 1], axis=0) * depth_both, axis=0)
    part_im = jnp.sum(jnp.sum(lre * spread[:, 1] + lim * spread[:, 0], axis=0) * depth_both, axis=0)
    part = jnp.stack([part_re, part_im]).reshape(2, 2, pols, quarter)
    part = jnp.where(owner_index == 0, part, part[:, ::-1])
    outgoing = jnp.transpose(part, (2, 1, 0, 3)).reshape(pols * owners, 2 * quarter)
    incoming = lax.all_to_all(outgoing, ("pol", "tm"), split_axis=0, concat_axis=0, tiled=True)
    pred = jnp.sum(incoming.reshape(pols, owners, 2, quarter), axis=1)

    slot_index = lax.axis_index("pol") * quarter + jnp.arange(quarter, dtype=jnp.int32)
    block_table = visibility_groups_table.reshape(3, visibility_groups_table.shape[3])
    slot_live, channel, baseline, member = decode_slots(block_table, slot_index)
    stations = jnp.take(antenna_links, baseline, axis=1)
    channel_gains = jnp.take(complex_receiver_factors, block_table[0], axis=0)
    blocks = block_table.shape[1]
    pick = (
        stations.reshape(2 * quarter)[:, None] == jnp.arange(NST, dtype=jnp.int32)[None, :]
    ).astype(jnp.float32)
    gains = nt_dot(channel_gains.reshape(blocks * 4, NST), pick, precision=exact)
    gains = gains.reshape(blocks, 4, 2, quarter)
    weight = jnp.transpose(member).astype(jnp.float32)[:, None, None, :]
    gains = jnp.sum(gains * weight, axis=0)
    observed = measured_correlations.reshape(NPOL, 2, quarter)
    resid_re, resid_im, leading, trailing = model_terms(
        pred[:, 0], pred[:, 1], observed[:, 0], observed[:, 1], gains[:, 0], gains[:, 1], slot_live
    )
    residual = jnp.stack([resid_re, resid_im], axis=1).reshape(1, 2 * NPOL, 1, quarter)

    everyone = ("facet", "pol", "tm")
    total = lax.axis_size(everyone)
    idents = jnp.concatenate([stations, channel[None]], axis=0).astype(jnp.float32)
    records = jnp.concatenate([idents, leading, trailing], axis=0).reshape(1, 11 * quarter)
    sent = jnp.broadcast_to(records, (total, 11 * quarter))
    piece = lax.all_to_all(sent, everyone, split_axis=0, concat_axis=0, tiled=True)
    piece = jnp.transpose(piece.reshape(total, 11, quarter), (1, 0, 2)).reshape(11, total * quarter)
    own_count = NST // total
    mine = (
        lax.axis_index(everyone) * own_count + jnp.arange(own_count, dtype=jnp.int32)
    ).astype(jnp.float32)
    match_first = (mine[:, None] == piece[0][None, :]).astype(jnp.float32)
    match_second = (mine[:, None] == piece[1][None, :]).astype(jnp.float32)
    weighted = match_first[:, None, :] * piece[None, 3:7] + match_second[:, None, :] * piece[None, 7:11]
    onehot = (
        jnp.arange(NCH, dtype=jnp.int32).astype(jnp.float32)[:, None] == piece[2][None, :]
    ).astype(jnp.float32)
    summed = nt_dot(
        weighted.reshape(own_count * 4, total * quarter), onehot, precision=lax.Precision.HIGH
    )
    gain_grad = grad_scale * jnp.transpose(
        summed.reshape(own_count, 4, NCH), (0, 2, 1)
    ).reshape(own_count, 4 * NCH)
    return residual, gain_grad


def solution(mesh):
    return jax.shard_map(
        on_device,
        mesh=mesh,
        in_specs=(
            P("facet", "pol", None, "tm", None),
            P("facet", "tm", None, None),
            P("facet", "tm", None, None),
            P("facet", "tm", None, None),
            P("facet", None, "tm", "pol"),
            P("facet", "tm", None, None),
            P(),
            P(),
        ),
        out_specs=(P("facet", None, "tm", "pol"), P(("facet", "pol", "tm"), None)),
        check_vma=False,
    )
```

```python
import functools
import math

import jax
import jax.numpy as jnp
import numpy as np
from jax import lax
from jax.experimental import pallas as pl
from jax.experimental.pallas import tpu as pltpu
from jax.sharding import PartitionSpec as P

FGRID = 8
FS = 4096
MC = 64
SG = 512
NPOL = 4
NW = 2
NCH = 256
NST = 512
CHUNK = 512

w_chirp = 0.37
grad_scale = 0.1
feed_first = np.array([0, 0, 1, 1])
feed_second = np.array([0, 1, 0, 1])


def unit_angles(left, right, length):
    product = np.outer(np.arange(left), np.arange(right)) % length
    return 2.0 * math.pi * product / length


def fourier_factors(subgrids):
    spread = FS // MC
    alpha = unit_angles(FS // spread, MC, MC)
    p = np.concatenate([np.cos(alpha), -np.sin(alpha)], axis=1) / math.sqrt(FS)
    q = np.concatenate([-np.sin(alpha), -np.cos(alpha)], axis=1) / math.sqrt(FS)
    beta = unit_angles(spread, subgrids * MC, FS).reshape(spread, subgrids, 1, MC)
    beta = np.broadcast_to(beta, (spread, subgrids, 2, MC)).reshape(spread, subgrids * 2 * MC)
    tile = lambda t: np.tile(t, (1, subgrids)).astype(np.float32)
    return (
        tile(p),
        tile(q),
        np.cos(beta).astype(np.float32),
        np.sin(beta).astype(np.float32),
    )


def fourier_kernel(p_ref, q_ref, c_ref, s_ref, x_ref, o_ref, table, total):
    step = pl.program_id(0)
    facets, _, rows, chunk = x_ref.shape
    subgrids = o_ref.shape[0]
    spread = c_ref.shape[0]
    cosine, sine = c_ref[...], s_ref[...]
    for part in range(chunk // spread):
        lead = p_ref[part : part + 1, :]
        other = q_ref[part : part + 1, :]
        table[part * spread : (part + 1) * spread, :] = (lead * cosine + other * sine).astype(
            jnp.bfloat16
        )
    x = x_ref[...].reshape(facets * 2 * rows, chunk)
    product = jnp.dot(x, table[...], preferred_element_type=jnp.float32)

    @pl.when(step == 0)
    def _():
        total[...] = product

    @pl.when(step > 0)
    def _():
        total[...] += product

    @pl.when(step == pl.num_programs(0) - 1)
    def _():
        lane = lax.broadcasted_iota(jnp.int32, (rows, 2 * MC), 1)
        sign = jnp.where(lane < MC, -1.0, 1.0)
        packed = o_ref.shape[3] // (2 * MC)
        for f in range(facets):
            for s in range(subgrids):
                cut = slice(s * 2 * MC, (s + 1) * 2 * MC)
                first = total[2 * f * rows : (2 * f + 1) * rows, cut]
                second = total[(2 * f + 1) * rows : (2 * f + 2) * rows, cut]
                value = first + sign * pltpu.roll(second, MC, 1)
                j = f % packed
                o_ref[s, f // packed, :, j * 2 * MC : (j + 1) * 2 * MC] = value.astype(jnp.bfloat16)


def fourier(x, subgrids):
    facets, _, rows, length = x.shape
    width = subgrids * 2 * MC
    spread = FS // MC
    packed = FGRID if facets % FGRID == 0 else 1
    per_step = CHUNK // spread
    factors = [jnp.asarray(t) for t in fourier_factors(subgrids)]
    return pl.pallas_call(
        fourier_kernel,
        out_shape=jax.ShapeDtypeStruct(
            (subgrids, facets // packed, rows, packed * 2 * MC), jnp.bfloat16
        ),
        grid=(length // CHUNK,),
        in_specs=[
            pl.BlockSpec((per_step, width), lambda g: (g, 0)),
            pl.BlockSpec((per_step, width), lambda g: (g, 0)),
            pl.BlockSpec((spread, width), lambda g: (0, 0)),
            pl.BlockSpec((spread, width), lambda g: (0, 0)),
            pl.BlockSpec((facets, 2, rows, CHUNK), lambda g: (0, 0, 0, g)),
        ],
        out_specs=pl.BlockSpec(
            (subgrids, facets // packed, rows, packed * 2 * MC), lambda g: (0, 0, 0, 0)
        ),
        scratch_shapes=[
            pltpu.VMEM((CHUNK, width), jnp.bfloat16),
            pltpu.VMEM((facets * 2 * rows, width), jnp.float32),
        ],
        compiler_params=pltpu.CompilerParams(
            dimension_semantics=("arbitrary",), vmem_limit_bytes=48 << 20
        ),
    )(*factors, x)


def subgrid_tables():
    angle = unit_angles(SG, SG, SG)
    re = np.cos(angle) / math.sqrt(SG)
    im = np.sin(angle) / math.sqrt(SG)
    blocks = lambda t: t.reshape(SG, FGRID, MC)
    second = np.stack([blocks(re), -blocks(im)], axis=2).reshape(SG, 2 * SG)
    third = np.stack([blocks(im), blocks(re)], axis=2).reshape(SG, 2 * SG)
    return [t.astype(jnp.bfloat16) for t in (re, im, second, third)]


def chirp_line():
    offset = np.arange(SG) - SG // 2
    angle = 2.0 * math.pi * w_chirp * (offset * offset) / float(SG * SG)
    return np.cos(angle).astype(np.float32), np.sin(angle).astype(np.float32)


def chirped(taper):
    cosine, sine = chirp_line()
    wide = taper.astype(jnp.float32)
    return jnp.concatenate(
        [taper, (wide * cosine).astype(jnp.bfloat16), (wide * sine).astype(jnp.bfloat16)], axis=0
    )


def decode_slots(block_table, slot_index):
    channels = block_table[0]
    offsets = block_table[1]
    amounts = block_table[2]
    starts = jnp.cumsum(amounts) - amounts
    relative = slot_index[:, None] - starts[None, :]
    member = ((relative >= 0) & (relative < amounts[None, :])).astype(jnp.int32)
    slot_live = jnp.sum(member, axis=-1)
    channel = jnp.sum(member * channels[None, :], axis=-1)
    baseline = jnp.sum(member * (offsets[None, :] + relative), axis=-1)
    return slot_live, channel, baseline, member


def model_terms(pred_re, pred_im, obs_re, obs_im, gain_first, gain_second, slot_live):
    first_re = gain_first[2 * feed_first]
    first_im = gain_first[2 * feed_first + 1]
    second_re = gain_second[2 * feed_second]
    second_im = gain_second[2 * feed_second + 1]
    both_re = first_re * second_re + first_im * second_im
    both_im = first_im * second_re - first_re * second_im
    model_re = both_re * pred_re - both_im * pred_im
    model_im = both_re * pred_im + both_im * pred_re
    alive_mask = slot_live.astype(jnp.float32)[None, :]
    resid_re = alive_mask * (obs_re - model_re)
    resid_im = alive_mask * (obs_im - model_im)
    cross_re = second_re * pred_re + second_im * pred_im
    cross_im = second_im * pred_re - second_re * pred_im
    lead_re = -(resid_re * cross_re - resid_im * cross_im)
    lead_im = -(resid_re * cross_im + resid_im * cross_re)
    along_re = first_re * pred_re - first_im * pred_im
    along_im = first_re * pred_im + first_im * pred_re
    trail_re = -(resid_re * along_re + resid_im * along_im)
    trail_im = -(resid_re * along_im - resid_im * along_re)
    leading = jnp.stack(
        [
            lead_re[0] + lead_re[1],
            lead_im[0] + lead_im[1],
            lead_re[2] + lead_re[3],
            lead_im[2] + lead_im[3],
        ]
    )
    trailing = jnp.stack(
        [
            trail_re[0] + trail_re[2],
            trail_im[0] + trail_im[2],
            trail_re[1] + trail_re[3],
            trail_im[1] + trail_im[3],
        ]
    )
    return resid_re, resid_im, leading, trailing


def nt_dot(left, right, **kw):
    return lax.dot_general(
        left, right, (((1,), (1,)), ((), ())), preferred_element_type=jnp.float32, **kw
    )


def on_device(
    tile_spectral_lines,
    taper_leading_axis,
    taper_trailing_axis,
    depth_layer_factors,
    measured_correlations,
    visibility_groups_table,
    antenna_links,
    complex_receiver_factors,
):
    exact = lax.Precision.HIGHEST
    subgrids = lax.axis_size("facet")
    owners = lax.axis_size("tm")
    pols = lax.axis_size("pol")
    owner_index = lax.axis_index("tm")
    slots = taper_leading_axis.shape[2]
    quarter = measured_correlations.shape[3]
    rows = tile_spectral_lines.shape[3]

    tapers = jnp.concatenate(
        [
            taper_leading_axis.reshape(slots, SG),
            taper_trailing_axis.reshape(slots, SG),
        ],
        axis=1,
    )
    partner = lax.ppermute(tapers, "tm", [(0, 1), (1, 0)])
    depth = depth_layer_factors.reshape(NW, slots)
    depth_partner = lax.ppermute(depth, "tm", [(0, 1), (1, 0)])
    both = jnp.concatenate([tapers, partner], axis=0)
    depth_both = jnp.concatenate([depth, depth_partner], axis=1).astype(jnp.float32)

    contrib = fourier(tile_spectral_lines[:, 0], subgrids)
    received = lax.all_to_all(contrib, "facet", split_axis=0, concat_axis=1, tiled=True)
    if received.shape[3] == 2 * SG:
        lines = received.reshape(FGRID * rows, 2 * SG)
    else:
        lines = jnp.transpose(
            received.reshape(FGRID, FGRID, rows, 2 * MC), (0, 2, 1, 3)
        ).reshape(FGRID * rows, 2 * SG)

    table_re, table_im, second, third = [jnp.asarray(t) for t in subgrid_tables()]
    own = 2 * slots
    trail3 = chirped(both[:, SG:])
    right_a = jnp.dot(trail3, second, preferred_element_type=jnp.float32).reshape(3, own, 2 * SG)
    right_b = jnp.dot(trail3, third, preferred_element_type=jnp.float32).reshape(3, own, 2 * SG)
    right = jnp.stack(
        [
            right_a[0],
            right_a[1] - right_b[2],
            right_b[0],
            right_b[1] + right_a[2],
        ]
    ).astype(jnp.bfloat16)
    lead3 = chirped(both[:, :SG])

    def own_rows(table):
        return lax.dynamic_index_in_dim(
            table.reshape(FGRID, owners, rows, SG), owner_index, 1, keepdims=False
        ).reshape(FGRID * rows, SG)

    left_re = nt_dot(own_rows(table_re), lead3).reshape(FGRID * rows, 3, own)
    left_im = nt_dot(own_rows(table_im), lead3).reshape(FGRID * rows, 3, own)
    lre = jnp.stack([left_re[:, 0], left_re[:, 1] - left_im[:, 2]], axis=1)
    lim = jnp.stack([left_im[:, 0], left_re[:, 2] + left_im[:, 1]], axis=1)
    spread = nt_dot(lines, right.reshape(4 * own, 2 * SG)).reshape(FGRID * rows, 2, 2, own)
    part_re = jnp.sum(jnp.sum(lre * spread[:, 0] - lim * spread[:, 1], axis=0) * depth_both, axis=0)
    part_im = jnp.sum(jnp.sum(lre * spread[:, 1] + lim * spread[:, 0], axis=0) * depth_both, axis=0)
    part = jnp.stack([part_re, part_im]).reshape(2, 2, pols, quarter)
    part = jnp.where(owner_index == 0, part, part[:, ::-1])
    outgoing = jnp.transpose(part, (2, 1, 0, 3)).reshape(pols * owners, 2 * quarter)
    incoming = lax.all_to_all(outgoing, ("pol", "tm"), split_axis=0, concat_axis=0, tiled=True)
    pred = jnp.sum(incoming.reshape(pols, owners, 2, quarter), axis=1)

    slot_index = lax.axis_index("pol") * quarter + jnp.arange(quarter, dtype=jnp.int32)
    block_table = visibility_groups_table.reshape(3, visibility_groups_table.shape[3])
    slot_live, channel, baseline, member = decode_slots(block_table, slot_index)
    stations = jnp.stack(
        [jnp.take(antenna_links[0], baseline), jnp.take(antenna_links[1], baseline)]
    )
    channel_gains = jnp.take(complex_receiver_factors, block_table[0], axis=0)
    blocks = block_table.shape[1]
    pick = (
        stations.reshape(2 * quarter)[:, None] == jnp.arange(NST, dtype=jnp.int32)[None, :]
    ).astype(jnp.float32)
    gains = nt_dot(channel_gains.reshape(blocks * 4, NST), pick, precision=exact)
    gains = gains.reshape(blocks, 4, 2, quarter)
    weight = jnp.transpose(member).astype(jnp.float32)[:, None, None, :]
    gains = jnp.sum(gains * weight, axis=0)
    observed = measured_correlations.reshape(NPOL, 2, quarter)
    resid_re, resid_im, leading, trailing = model_terms(
        pred[:, 0], pred[:, 1], observed[:, 0], observed[:, 1], gains[:, 0], gains[:, 1], slot_live
    )
    residual = jnp.stack([resid_re, resid_im], axis=1).reshape(1, 2 * NPOL, 1, quarter)

    everyone = ("facet", "pol", "tm")
    total = lax.axis_size(everyone)
    idents = jnp.concatenate([stations, channel[None]], axis=0).astype(jnp.float32)
    records = jnp.concatenate([idents, leading, trailing], axis=0).reshape(1, 11 * quarter)
    sent = jnp.broadcast_to(records, (total, 11 * quarter))
    piece = lax.all_to_all(sent, everyone, split_axis=0, concat_axis=0, tiled=True)
    piece = jnp.transpose(piece.reshape(total, 11, quarter), (1, 0, 2)).reshape(11, total * quarter)
    own_count = NST // total
    mine = (
        lax.axis_index(everyone) * own_count + jnp.arange(own_count, dtype=jnp.int32)
    ).astype(jnp.float32)
    match_first = (mine[:, None] == piece[0][None, :]).astype(jnp.float32)
    match_second = (mine[:, None] == piece[1][None, :]).astype(jnp.float32)
    weighted = match_first[:, None, :] * piece[None, 3:7] + match_second[:, None, :] * piece[None, 7:11]
    onehot = (
        jnp.arange(NCH, dtype=jnp.int32).astype(jnp.float32)[:, None] == piece[2][None, :]
    ).astype(jnp.float32)
    summed = nt_dot(
        weighted.reshape(own_count * 4, total * quarter), onehot, precision=lax.Precision.HIGH
    )
    gain_grad = grad_scale * jnp.transpose(
        summed.reshape(own_count, 4, NCH), (0, 2, 1)
    ).reshape(own_count, 4 * NCH)
    return residual, gain_grad


def solution(mesh):
    return jax.shard_map(
        on_device,
        mesh=mesh,
        in_specs=(
            P("facet", "pol", None, "tm", None),
            P("facet", "tm", None, None),
            P("facet", "tm", None, None),
            P("facet", "tm", None, None),
            P("facet", None, "tm", "pol"),
            P("facet", "tm", None, None),
            P(),
            P(),
        ),
        out_specs=(P("facet", None, "tm", "pol"), P(("facet", "pol", "tm"), None)),
        check_vma=False,
    )
```

```python
import functools
import math

import jax
import jax.numpy as jnp
import numpy as np
from jax import lax
from jax.experimental import pallas as pl
from jax.experimental.pallas import tpu as pltpu
from jax.sharding import PartitionSpec as P

FGRID = 8
FS = 4096
MC = 64
SG = 512
NPOL = 4
NW = 2
NCH = 256
NST = 512
CHUNK = 512

w_chirp = 0.37
grad_scale = 0.1


def unit_angles(left, right, length):
    product = np.outer(np.arange(left), np.arange(right)) % length
    return 2.0 * math.pi * product / length


def fourier_factors(subgrids):
    spread = FS // MC
    alpha = unit_angles(FS // spread, MC, MC)
    p = np.concatenate([np.cos(alpha), -np.sin(alpha)], axis=1) / math.sqrt(FS)
    q = np.concatenate([-np.sin(alpha), -np.cos(alpha)], axis=1) / math.sqrt(FS)
    beta = unit_angles(spread, subgrids * MC, FS).reshape(spread, subgrids, 1, MC)
    beta = np.broadcast_to(beta, (spread, subgrids, 2, MC)).reshape(spread, subgrids * 2 * MC)
    tile = lambda t: np.tile(t, (1, subgrids)).astype(np.float32)
    return (
        tile(p),
        tile(q),
        np.cos(beta).astype(np.float32),
        np.sin(beta).astype(np.float32),
    )


def fourier_kernel(p_ref, q_ref, c_ref, s_ref, x_ref, o_ref, table, total):
    step = pl.program_id(0)
    facets, _, rows, chunk = x_ref.shape
    subgrids = o_ref.shape[0]
    spread = c_ref.shape[0]
    cosine, sine = c_ref[...], s_ref[...]
    for part in range(chunk // spread):
        lead = p_ref[part : part + 1, :]
        other = q_ref[part : part + 1, :]
        table[part * spread : (part + 1) * spread, :] = (lead * cosine + other * sine).astype(
            jnp.bfloat16
        )
    x = x_ref[...].reshape(facets * 2 * rows, chunk)
    product = jnp.dot(x, table[...], preferred_element_type=jnp.float32)

    @pl.when(step == 0)
    def _():
        total[...] = product

    @pl.when(step > 0)
    def _():
        total[...] += product

    @pl.when(step == pl.num_programs(0) - 1)
    def _():
        lane = lax.broadcasted_iota(jnp.int32, (rows, 2 * MC), 1)
        sign = jnp.where(lane < MC, -1.0, 1.0)
        packed = o_ref.shape[3] // (2 * MC)
        for f in range(facets):
            for s in range(subgrids):
                cut = slice(s * 2 * MC, (s + 1) * 2 * MC)
                first = total[2 * f * rows : (2 * f + 1) * rows, cut]
                second = total[(2 * f + 1) * rows : (2 * f + 2) * rows, cut]
                value = first + sign * pltpu.roll(second, MC, 1)
                j = f % packed
                o_ref[s, f // packed, :, j * 2 * MC : (j + 1) * 2 * MC] = value.astype(jnp.bfloat16)


def fourier(x, subgrids):
    facets, _, rows, length = x.shape
    width = subgrids * 2 * MC
    spread = FS // MC
    packed = FGRID if facets % FGRID == 0 else 1
    per_step = CHUNK // spread
    factors = [jnp.asarray(t) for t in fourier_factors(subgrids)]
    return pl.pallas_call(
        fourier_kernel,
        out_shape=jax.ShapeDtypeStruct(
            (subgrids, facets // packed, rows, packed * 2 * MC), jnp.bfloat16
        ),
        grid=(length // CHUNK,),
        in_specs=[
            pl.BlockSpec((per_step, width), lambda g: (g, 0)),
            pl.BlockSpec((per_step, width), lambda g: (g, 0)),
            pl.BlockSpec((spread, width), lambda g: (0, 0)),
            pl.BlockSpec((spread, width), lambda g: (0, 0)),
            pl.BlockSpec((facets, 2, rows, CHUNK), lambda g: (0, 0, 0, g)),
        ],
        out_specs=pl.BlockSpec(
            (subgrids, facets // packed, rows, packed * 2 * MC), lambda g: (0, 0, 0, 0)
        ),
        scratch_shapes=[
            pltpu.VMEM((CHUNK, width), jnp.bfloat16),
            pltpu.VMEM((facets * 2 * rows, width), jnp.float32),
        ],
        compiler_params=pltpu.CompilerParams(
            dimension_semantics=("arbitrary",), vmem_limit_bytes=48 << 20
        ),
    )(*factors, x)


def subgrid_tables():
    angle = unit_angles(SG, SG, SG)
    re = np.cos(angle) / math.sqrt(SG)
    im = np.sin(angle) / math.sqrt(SG)
    blocks = lambda t: t.reshape(SG, FGRID, MC)
    second = np.stack([blocks(re), -blocks(im)], axis=2).reshape(SG, 2 * SG)
    third = np.stack([blocks(im), blocks(re)], axis=2).reshape(SG, 2 * SG)
    return [t.astype(jnp.bfloat16) for t in (re, im, second, third)]


def chirp_line():
    offset = np.arange(SG) - SG // 2
    angle = 2.0 * math.pi * w_chirp * (offset * offset) / float(SG * SG)
    return np.cos(angle).astype(np.float32), np.sin(angle).astype(np.float32)


def decode_slots(block_table, slot_index):
    channels = block_table[0]
    offsets = block_table[1]
    amounts = block_table[2]
    starts = jnp.cumsum(amounts) - amounts
    relative = slot_index[:, None] - starts[None, :]
    member = ((relative >= 0) & (relative < amounts[None, :])).astype(jnp.int32)
    slot_live = jnp.sum(member, axis=-1)
    channel = jnp.sum(member * channels[None, :], axis=-1)
    baseline = jnp.sum(member * (offsets[None, :] + relative), axis=-1)
    return slot_live, channel, baseline, member


def model_terms(pred, observed, first, second, alive):
    residual, lead, trail = [], [], []
    for p in range(NPOL):
        f1, f2 = p // 2, p % 2
        pred_re, pred_im = pred[p]
        first_re, first_im = first[2 * f1], first[2 * f1 + 1]
        second_re, second_im = second[2 * f2], second[2 * f2 + 1]
        both_re = first_re * second_re + first_im * second_im
        both_im = first_im * second_re - first_re * second_im
        resid_re = alive * (observed[2 * p] - (both_re * pred_re - both_im * pred_im))
        resid_im = alive * (observed[2 * p + 1] - (both_re * pred_im + both_im * pred_re))
        cross_re = second_re * pred_re + second_im * pred_im
        cross_im = second_im * pred_re - second_re * pred_im
        along_re = first_re * pred_re - first_im * pred_im
        along_im = first_re * pred_im + first_im * pred_re
        residual += [resid_re, resid_im]
        lead.append(
            (-(resid_re * cross_re - resid_im * cross_im), -(resid_re * cross_im + resid_im * cross_re))
        )
        trail.append(
            (-(resid_re * along_re + resid_im * along_im), -(resid_re * along_im - resid_im * along_re))
        )
    leading = [lead[2 * f][r] + lead[2 * f + 1][r] for f in range(2) for r in range(2)]
    trailing = [trail[f][r] + trail[f + 2][r] for f in range(2) for r in range(2)]
    return residual, leading, trailing


def nt_dot(left, right, **kw):
    return lax.dot_general(
        left, right, (((1,), (1,)), ((), ())), preferred_element_type=jnp.float32, **kw
    )


def chirped_rows(taper, chirp_ref):
    wide = taper.astype(jnp.float32)
    return jnp.concatenate(
        [
            taper,
            (wide * chirp_ref[0:1, :]).astype(jnp.bfloat16),
            (wide * chirp_ref[1:2, :]).astype(jnp.bfloat16),
        ],
        axis=0,
    )


def predict_kernel(
    sizes,
    contrib_ref,
    lead_ref,
    trail_ref,
    depth_ref,
    observed_ref,
    gains_ref,
    idents_ref,
    table_re_ref,
    table_im_ref,
    second_ref,
    third_ref,
    chirp_ref,
    residual_ref,
    grad_ref,
    got,
    lines,
    tapers,
    right,
    left,
    part_out,
    part_in,
    observed_in,
    record_out,
    record_in,
    got_send,
    got_recv,
    taper_send,
    taper_recv,
    observed_send,
    observed_recv,
    part_send,
    part_recv,
    record_send,
    record_recv,
):
    subgrids, pols, owners = sizes
    z, p, t = lax.axis_index("facet"), lax.axis_index("pol"), lax.axis_index("tm")
    slots = lead_ref.shape[0]
    _, groups, rows, width = contrib_ref.shape
    mesh_id = pl.DeviceIdType.MESH

    def remote(src, dst, send, recv, peer):
        return pltpu.make_async_remote_copy(
            src_ref=src,
            dst_ref=dst,
            send_sem=send,
            recv_sem=recv,
            device_id=peer,
            device_id_type=mesh_id,
        )

    across_total = subgrids * owners
    plane_total = pols * owners
    across = z * owners + t
    plane = p * owners + t

    def across_peer(d):
        other = lax.rem(across + d, across_total)
        return other, (other // owners, p, lax.rem(other, owners))

    def plane_peer(d):
        other = lax.rem(plane + d, plane_total)
        return other, (z, other // owners, lax.rem(other, owners))

    barrier = pltpu.get_barrier_semaphore()
    for d in range(1, across_total):
        pl.semaphore_signal(barrier, inc=1, device_id=across_peer(d)[1], device_id_type=mesh_id)
    for d in range(1, pols):
        q = lax.rem(p + d, pols)
        for o in range(owners):
            pl.semaphore_signal(barrier, inc=1, device_id=(z, q, o), device_id_type=mesh_id)
    pl.semaphore_wait(barrier, across_total - 1 + (pols - 1) * owners)

    copies = []
    for d in range(1, subgrids):
        other = lax.rem(z + d, subgrids)
        copies.append(
            remote(contrib_ref.at[other], got.at[z], got_send.at[d], got_recv.at[d], (other, p, t))
        )
    partner = lax.rem(t + 1, owners)
    taper_copies = [
        remote(ref, tapers.at[t, k], taper_send.at[k], taper_recv.at[k], (z, p, partner))
        for k, ref in enumerate((trail_ref, lead_ref))
    ]
    observed_copies = []
    for d in range(1, pols):
        q = lax.rem(p + d, pols)
        observed_copies.append(
            remote(
                observed_ref, observed_in.at[p], observed_send.at[d], observed_recv.at[d], (z, q, t)
            )
        )
    for copy in copies + taper_copies + observed_copies:
        copy.start()

    table_re = jnp.concatenate([table_re_ref[i, t] for i in range(FGRID)], axis=0)
    table_im = jnp.concatenate([table_im_ref[i, t] for i in range(FGRID)], axis=0)

    def prepare(owner, trail, lead):
        trail3 = chirped_rows(trail, chirp_ref)
        a = jnp.dot(trail3, second_ref[...], preferred_element_type=jnp.float32)
        b = jnp.dot(trail3, third_ref[...], preferred_element_type=jnp.float32)
        n0, n1, n2 = slice(0, slots), slice(slots, 2 * slots), slice(2 * slots, 3 * slots)
        right[owner, 0:slots, :] = a[n0].astype(jnp.bfloat16)
        right[owner, slots : 2 * slots, :] = (a[n1] - b[n2]).astype(jnp.bfloat16)
        right[owner, 2 * slots : 3 * slots, :] = b[n0].astype(jnp.bfloat16)
        right[owner, 3 * slots : 4 * slots, :] = (b[n1] + a[n2]).astype(jnp.bfloat16)
        lead3 = chirped_rows(lead, chirp_ref)
        u = nt_dot(table_re, lead3)
        v = nt_dot(table_im, lead3)
        left[owner, 0] = u[:, n0]
        left[owner, 1] = v[:, n0]
        left[owner, 2] = u[:, n1] - v[:, n2]
        left[owner, 3] = u[:, n2] + v[:, n1]

    prepare(t, trail_ref[...], lead_ref[...])
    got[z] = contrib_ref[z]
    for copy in taper_copies:
        copy.wait()
    prepare(partner, tapers[partner, 0], tapers[partner, 1])
    for copy in copies:
        copy.wait()
    if width == 2 * SG:
        whole = got[...].reshape(subgrids * groups * rows, width)
    else:
        for f in range(subgrids * groups):
            i, j = f // FGRID, f % FGRID
            lines[i * rows : (i + 1) * rows, j * 2 * MC : (j + 1) * 2 * MC] = got[
                f // groups, f % groups
            ]
        whole = lines[...]
    for o in range(owners):
        spread = nt_dot(whole, right[o])
        for w in range(NW):
            g_re = spread[:, w * slots : (w + 1) * slots]
            g_im = spread[:, (NW + w) * slots : (NW + w + 1) * slots]
            l_re, l_im = left[o, 2 * w], left[o, 2 * w + 1]
            part_out[o, 2 * w : 2 * w + 1, :] = jnp.sum(l_re * g_re - l_im * g_im, axis=0, keepdims=True)
            part_out[o, 2 * w + 1 : 2 * w + 2, :] = jnp.sum(
                l_re * g_im + l_im * g_re, axis=0, keepdims=True
            )
        part_out[o, 2 * NW :, :] = jnp.zeros((8 - 2 * NW, slots), jnp.float32)

    part_copies = []
    for d in range(1, plane_total):
        other, peer = plane_peer(d)
        part_copies.append(
            remote(
                part_out.at[lax.rem(other, owners)],
                part_in.at[plane],
                part_send.at[d],
                part_recv.at[d],
                peer,
            )
        )
    for copy in part_copies:
        copy.start()
    part_in[plane] = part_out[t]
    observed_in[p] = observed_ref[...]
    for copy in observed_copies:
        copy.wait()
    observed = observed_in[0]
    for q in range(1, pols):
        observed = observed + observed_in[q]
    depth = depth_ref[...].astype(jnp.float32)
    for copy in part_copies:
        copy.wait()

    pred = []
    per_pol = part_in.shape[0] // NPOL
    for q in range(NPOL):
        block = part_in[q * per_pol]
        for o in range(1, per_pol):
            block = block + part_in[q * per_pol + o]
        pred.append(
            tuple(
                sum(depth[w : w + 1] * block[2 * w + c : 2 * w + c + 1] for w in range(NW))
                for c in range(2)
            )
        )
    gains = gains_ref[...]
    idents = idents_ref[...]
    residual, leading, trailing = model_terms(
        pred,
        [observed[k : k + 1] for k in range(2 * NPOL)],
        [gains[k : k + 1] for k in range(4)],
        [gains[4 + k : 5 + k] for k in range(4)],
        idents[3:4],
    )
    for k in range(3):
        record_out[k : k + 1, :] = idents[k : k + 1]
    for k in range(4):
        record_out[3 + k : 4 + k, :] = leading[k]
        record_out[7 + k : 8 + k, :] = trailing[k]
    record_out[11:, :] = jnp.zeros((5, slots), jnp.float32)
    record_copies = []
    for d in range(1, across_total):
        other, peer = across_peer(d)
        record_copies.append(
            remote(record_out, record_in.at[across], record_send.at[d], record_recv.at[d], peer)
        )
    for copy in record_copies:
        copy.start()
    record_in[across] = record_out[...]
    for k in range(2 * NPOL):
        residual_ref[k : k + 1, :] = residual[k]
    for copy in record_copies:
        copy.wait()

    piece = jnp.concatenate([record_in[d] for d in range(across_total)], axis=1)
    own_count = grad_ref.shape[1]
    index = (z * pols + p) * owners + t
    mine = (index * own_count + lax.broadcasted_iota(jnp.int32, (own_count, 1), 0)).astype(
        jnp.float32
    )
    match_first = mine == piece[0:1]
    match_second = mine == piece[1:2]
    weighted = jnp.concatenate(
        [
            jnp.where(match_first, piece[3 + k : 4 + k], 0.0)
            + jnp.where(match_second, piece[7 + k : 8 + k], 0.0)
            for k in range(4)
        ],
        axis=0,
    )
    high = weighted.astype(jnp.bfloat16)
    low = (weighted - high.astype(jnp.float32)).astype(jnp.bfloat16)
    channel_ids = lax.broadcasted_iota(jnp.int32, (NCH, 1), 0).astype(jnp.float32)
    onehot = jnp.where(channel_ids == piece[2:3], 1.0, 0.0).astype(jnp.bfloat16)
    summed = nt_dot(high, onehot) + nt_dot(low, onehot)
    for k in range(4):
        grad_ref[k] = grad_scale * summed[k * own_count : (k + 1) * own_count]


def predict(sizes, own_count, *operands):
    subgrids, pols, owners = sizes
    contrib, lead = operands[0], operands[1]
    _, groups, rows, width = contrib.shape
    slots = lead.shape[0]
    vmem = pl.BlockSpec(memory_space=pltpu.VMEM)
    dma = lambda n: pltpu.SemaphoreType.DMA((n,))
    across_total, plane_total = subgrids * owners, pols * owners
    return pl.pallas_call(
        functools.partial(predict_kernel, sizes),
        out_shape=(
            jax.ShapeDtypeStruct((2 * NPOL, slots), jnp.float32),
            jax.ShapeDtypeStruct((4, own_count, NCH), jnp.float32),
        ),
        in_specs=[vmem] * len(operands),
        out_specs=(vmem, vmem),
        scratch_shapes=[
            pltpu.VMEM(contrib.shape, jnp.bfloat16),
            pltpu.VMEM((FGRID * rows, 2 * SG), jnp.bfloat16),
            pltpu.VMEM((owners, 2, slots, SG), jnp.bfloat16),
            pltpu.VMEM((owners, 2 * NW * slots, 2 * SG), jnp.bfloat16),
            pltpu.VMEM((owners, 4, FGRID * rows, slots), jnp.float32),
            pltpu.VMEM((owners, 8, slots), jnp.float32),
            pltpu.VMEM((plane_total, 8, slots), jnp.float32),
            pltpu.VMEM((pols, 8, slots), jnp.float32),
            pltpu.VMEM((16, slots), jnp.float32),
            pltpu.VMEM((across_total, 16, slots), jnp.float32),
            dma(subgrids),
            dma(subgrids),
            dma(2),
            dma(2),
            dma(pols),
            dma(pols),
            dma(plane_total),
            dma(plane_total),
            dma(across_total),
            dma(across_total),
        ],
        compiler_params=pltpu.CompilerParams(
            collective_id=0, has_side_effects=True, vmem_limit_bytes=48 << 20
        ),
    )(*operands)


def on_device(
    tile_spectral_lines,
    taper_leading_axis,
    taper_trailing_axis,
    depth_layer_factors,
    measured_correlations,
    visibility_groups_table,
    antenna_links,
    complex_receiver_factors,
):
    exact = lax.Precision.HIGHEST
    sizes = tuple(lax.axis_size(name) for name in ("facet", "pol", "tm"))
    subgrids, pols, owners = sizes
    slots = taper_leading_axis.shape[2]
    quarter = measured_correlations.shape[3]
    rows = tile_spectral_lines.shape[3]
    pol_index = lax.axis_index("pol")

    slot_index = jnp.arange(slots, dtype=jnp.int32)
    block_table = visibility_groups_table.reshape(3, visibility_groups_table.shape[3])
    slot_live, channel, baseline, member = decode_slots(block_table, slot_index)
    stations = jnp.stack(
        [jnp.take(antenna_links[0], baseline), jnp.take(antenna_links[1], baseline)]
    )
    channel_gains = jnp.take(complex_receiver_factors, block_table[0], axis=0)
    blocks = block_table.shape[1]
    pick = (
        stations.reshape(2 * slots)[:, None] == jnp.arange(NST, dtype=jnp.int32)[None, :]
    ).astype(jnp.float32)
    gains = nt_dot(channel_gains.reshape(blocks * 4, NST), pick, precision=exact)
    gains = gains.reshape(blocks, 4, 2, slots)
    weight = jnp.transpose(member).astype(jnp.float32)[:, None, None, :]
    gains = jnp.sum(gains * weight, axis=0)
    gains = jnp.transpose(gains, (1, 0, 2)).reshape(8, slots)
    idents = jnp.concatenate(
        [stations, channel[None], slot_live[None], jnp.zeros((4, slots), jnp.int32)], axis=0
    ).astype(jnp.float32)

    observed = measured_correlations.reshape(2 * NPOL, quarter)
    in_quarter = (jnp.arange(slots, dtype=jnp.int32) // quarter == pol_index)[None, :]
    observed = jnp.where(in_quarter, jnp.tile(observed, (1, pols)), 0.0)

    contrib = fourier(tile_spectral_lines[:, 0], subgrids)
    table_re, table_im, second, third = [jnp.asarray(t) for t in subgrid_tables()]
    cosine, sine = chirp_line()
    own_count = NST // (subgrids * pols * owners)
    residual, grad = predict(
        sizes,
        own_count,
        contrib,
        taper_leading_axis.reshape(slots, SG),
        taper_trailing_axis.reshape(slots, SG),
        depth_layer_factors.reshape(NW, slots),
        observed,
        gains,
        idents,
        table_re.reshape(FGRID, owners, rows, SG),
        table_im.reshape(FGRID, owners, rows, SG),
        second,
        third,
        jnp.asarray(np.stack([cosine, sine])),
    )
    residual = lax.dynamic_slice_in_dim(residual, pol_index * quarter, quarter, 1)
    gain_grad = jnp.transpose(grad, (1, 2, 0)).reshape(own_count, 4 * NCH)
    return residual.reshape(1, 2 * NPOL, 1, quarter), gain_grad


def solution(mesh):
    return jax.shard_map(
        on_device,
        mesh=mesh,
        in_specs=(
            P("facet", "pol", None, "tm", None),
            P("facet", "tm", None, None),
            P("facet", "tm", None, None),
            P("facet", "tm", None, None),
            P("facet", None, "tm", "pol"),
            P("facet", "tm", None, None),
            P(),
            P(),
        ),
        out_specs=(P("facet", None, "tm", "pol"), P(("facet", "pol", "tm"), None)),
        check_vma=False,
    )
```

```python
import functools
import math

import jax
import jax.numpy as jnp
import numpy as np
from jax import lax
from jax.experimental import pallas as pl
from jax.experimental.pallas import tpu as pltpu
from jax.sharding import PartitionSpec as P

FGRID = 8
FS = 4096
MC = 64
SG = 512
NPOL = 4
NW = 2
NCH = 256
NST = 512
CHUNK = 512

w_chirp = 0.37
grad_scale = 0.1


def unit_angles(left, right, length):
    product = np.outer(np.arange(left), np.arange(right)) % length
    return 2.0 * math.pi * product / length


def fourier_factors(subgrids):
    spread = FS // MC
    alpha = unit_angles(FS // spread, MC, MC)
    p = np.concatenate([np.cos(alpha), -np.sin(alpha)], axis=1) / math.sqrt(FS)
    q = np.concatenate([-np.sin(alpha), -np.cos(alpha)], axis=1) / math.sqrt(FS)
    beta = unit_angles(spread, subgrids * MC, FS).reshape(spread, subgrids, 1, MC)
    beta = np.broadcast_to(beta, (spread, subgrids, 2, MC)).reshape(spread, subgrids * 2 * MC)
    tile = lambda t: np.tile(t, (1, subgrids)).astype(np.float32)
    return (
        tile(p),
        tile(q),
        np.cos(beta).astype(np.float32),
        np.sin(beta).astype(np.float32),
    )


def fetch_lookups(block_ref, links_ref, gain_ref, window, channel_gain, window_sem, gain_sem):
    blocks, _, span = window.shape
    copies = []
    for b in range(blocks):
        first = jnp.minimum(block_ref[1, b] // 128 * 128, links_ref.shape[1] - span)
        first = pl.multiple_of(first, 128)
        copies.append(
            pltpu.make_async_copy(
                links_ref.at[:, pl.ds(first, span)], window.at[b], window_sem.at[b]
            )
        )
        copies.append(
            pltpu.make_async_copy(
                gain_ref.at[block_ref[0, b]], channel_gain.at[b], gain_sem.at[b]
            )
        )
    return copies


def use_lookups(block_ref, links_ref, window, channel_gain, gains_ref, idents_ref):
    blocks, _, span = window.shape
    slots = idents_ref.shape[1]
    lane = lax.broadcasted_iota(jnp.int32, (1, slots), 1)
    place = lax.broadcasted_iota(jnp.int32, (span, slots), 0)
    lane_tall = lax.broadcasted_iota(jnp.int32, (span, slots), 1)
    begin = jnp.int32(0)
    member, picks = [], []
    channel = jnp.zeros((1, slots), jnp.float32)
    alive = jnp.zeros((1, slots), jnp.float32)
    for b in range(blocks):
        offset, amount = block_ref[1, b], block_ref[2, b]
        first = jnp.minimum(offset // 128 * 128, links_ref.shape[1] - span)
        inside = jnp.where((lane >= begin) & (lane < begin + amount), 1.0, 0.0)
        member.append(inside)
        alive += inside
        channel += inside * block_ref[0, b].astype(jnp.float32)
        hit = place == lane_tall + (offset - first - begin)
        picks.append((jnp.where(hit, 1.0, 0.0) * inside).astype(jnp.bfloat16))
        begin = begin + amount
    links = jnp.concatenate([window[b] for b in range(blocks)], axis=1)
    upper = links // 16
    lower = links - 16 * upper
    pieces = jnp.concatenate([upper, lower], axis=0).astype(jnp.float32).astype(jnp.bfloat16)
    found = jnp.dot(
        pieces, jnp.concatenate(picks, axis=0), preferred_element_type=jnp.float32
    )
    stations = 16.0 * found[0:2] + found[2:4]
    table = channel_gain[...].reshape(blocks * 4, channel_gain.shape[2])
    high = table.astype(jnp.bfloat16)
    rest = table - high.astype(jnp.float32)
    middle = rest.astype(jnp.bfloat16)
    low = (rest - middle.astype(jnp.float32)).astype(jnp.bfloat16)
    names = lax.broadcasted_iota(jnp.int32, (table.shape[1], 1), 0).astype(jnp.float32)
    for side in range(2):
        pick = jnp.where(names == stations[side : side + 1], 1.0, 0.0).astype(jnp.bfloat16)
        rows = (
            jnp.dot(high, pick, preferred_element_type=jnp.float32)
            + jnp.dot(middle, pick, preferred_element_type=jnp.float32)
            + jnp.dot(low, pick, preferred_element_type=jnp.float32)
        )
        chosen = member[0] * rows[0:4]
        for b in range(1, blocks):
            chosen = chosen + member[b] * rows[4 * b : 4 * b + 4]
        gains_ref[4 * side : 4 * side + 4, :] = chosen
    idents_ref[0:2, :] = stations
    idents_ref[2:3, :] = channel
    idents_ref[3:4, :] = alive
    idents_ref[4:8, :] = jnp.zeros((4, slots), jnp.float32)


def fourier_kernel(
    block_ref,
    links_ref,
    gain_ref,
    p_ref,
    q_ref,
    c_ref,
    s_ref,
    x_ref,
    o_ref,
    gains_ref,
    idents_ref,
    table,
    total,
    window,
    channel_gain,
    window_sem,
    gain_sem,
):
    step = pl.program_id(0)
    copies = fetch_lookups(
        block_ref, links_ref, gain_ref, window, channel_gain, window_sem, gain_sem
    )

    @pl.when(step == 0)
    def _():
        for copy in copies:
            copy.start()

    @pl.when(step == pl.num_programs(0) - 1)
    def _():
        for copy in copies:
            copy.wait()
        use_lookups(block_ref, links_ref, window, channel_gain, gains_ref, idents_ref)

    facets, _, rows, chunk = x_ref.shape
    subgrids = o_ref.shape[0]
    spread = c_ref.shape[0]
    cosine, sine = c_ref[...], s_ref[...]
    for part in range(chunk // spread):
        lead = p_ref[part : part + 1, :]
        other = q_ref[part : part + 1, :]
        table[part * spread : (part + 1) * spread, :] = (lead * cosine + other * sine).astype(
            jnp.bfloat16
        )
    x = x_ref[...].reshape(facets * 2 * rows, chunk)
    product = jnp.dot(x, table[...], preferred_element_type=jnp.float32)

    @pl.when(step == 0)
    def _():
        total[...] = product

    @pl.when(step > 0)
    def _():
        total[...] += product

    @pl.when(step == pl.num_programs(0) - 1)
    def _():
        lane = lax.broadcasted_iota(jnp.int32, (rows, 2 * MC), 1)
        sign = jnp.where(lane < MC, -1.0, 1.0)
        packed = o_ref.shape[3] // (2 * MC)
        for f in range(facets):
            for s in range(subgrids):
                cut = slice(s * 2 * MC, (s + 1) * 2 * MC)
                first = total[2 * f * rows : (2 * f + 1) * rows, cut]
                second = total[(2 * f + 1) * rows : (2 * f + 2) * rows, cut]
                value = first + sign * pltpu.roll(second, MC, 1)
                j = f % packed
                o_ref[s, f // packed, :, j * 2 * MC : (j + 1) * 2 * MC] = value.astype(jnp.bfloat16)


def fourier(x, subgrids, slots, block_table, links, station_gains):
    facets, _, rows, length = x.shape
    width = subgrids * 2 * MC
    spread = FS // MC
    packed = FGRID if facets % FGRID == 0 else 1
    per_step = CHUNK // spread
    blocks = block_table.shape[1]
    span = slots + 128
    in_place = lambda array: pltpu.with_memory_space_constraint(array, pltpu.HBM)
    factors = [in_place(jnp.asarray(t)) for t in fourier_factors(subgrids)]
    out = (subgrids, facets // packed, rows, packed * 2 * MC)
    return pl.pallas_call(
        fourier_kernel,
        out_shape=(
            jax.ShapeDtypeStruct(out, jnp.bfloat16),
            jax.ShapeDtypeStruct((8, slots), jnp.float32),
            jax.ShapeDtypeStruct((8, slots), jnp.float32),
        ),
        grid=(length // CHUNK,),
        in_specs=[
            pl.BlockSpec(memory_space=pltpu.SMEM),
            pl.BlockSpec(memory_space=pltpu.HBM),
            pl.BlockSpec(memory_space=pltpu.HBM),
            pl.BlockSpec((per_step, width), lambda g: (g, 0)),
            pl.BlockSpec((per_step, width), lambda g: (g, 0)),
            pl.BlockSpec((spread, width), lambda g: (0, 0)),
            pl.BlockSpec((spread, width), lambda g: (0, 0)),
            pl.BlockSpec((facets, 2, rows, CHUNK), lambda g: (0, 0, 0, g)),
        ],
        out_specs=(
            pl.BlockSpec(out, lambda g: (0, 0, 0, 0)),
            pl.BlockSpec((8, slots), lambda g: (0, 0)),
            pl.BlockSpec((8, slots), lambda g: (0, 0)),
        ),
        scratch_shapes=[
            pltpu.VMEM((CHUNK, width), jnp.bfloat16),
            pltpu.VMEM((facets * 2 * rows, width), jnp.float32),
            pltpu.VMEM((blocks, 2, span), jnp.int32),
            pltpu.VMEM((blocks, 4, NST), jnp.float32),
            pltpu.SemaphoreType.DMA((blocks,)),
            pltpu.SemaphoreType.DMA((blocks,)),
        ],
        compiler_params=pltpu.CompilerParams(
            dimension_semantics=("arbitrary",), vmem_limit_bytes=48 << 20
        ),
    )(
        block_table,
        in_place(links),
        in_place(station_gains),
        *factors,
        x,
    )


def subgrid_tables():
    angle = unit_angles(SG, SG, SG)
    re = np.cos(angle) / math.sqrt(SG)
    im = np.sin(angle) / math.sqrt(SG)
    blocks = lambda t: t.reshape(SG, FGRID, MC)
    second = np.stack([blocks(re), -blocks(im)], axis=2).reshape(SG, 2 * SG)
    third = np.stack([blocks(im), blocks(re)], axis=2).reshape(SG, 2 * SG)
    return [t.astype(jnp.bfloat16) for t in (re, im, second, third)]


def chirp_line():
    offset = np.arange(SG) - SG // 2
    angle = 2.0 * math.pi * w_chirp * (offset * offset) / float(SG * SG)
    return np.cos(angle).astype(np.float32), np.sin(angle).astype(np.float32)


def model_terms(pred, observed, first, second, alive):
    residual, lead, trail = [], [], []
    for p in range(NPOL):
        f1, f2 = p // 2, p % 2
        pred_re, pred_im = pred[p]
        first_re, first_im = first[2 * f1], first[2 * f1 + 1]
        second_re, second_im = second[2 * f2], second[2 * f2 + 1]
        both_re = first_re * second_re + first_im * second_im
        both_im = first_im * second_re - first_re * second_im
        resid_re = alive * (observed[2 * p] - (both_re * pred_re - both_im * pred_im))
        resid_im = alive * (observed[2 * p + 1] - (both_re * pred_im + both_im * pred_re))
        cross_re = second_re * pred_re + second_im * pred_im
        cross_im = second_im * pred_re - second_re * pred_im
        along_re = first_re * pred_re - first_im * pred_im
        along_im = first_re * pred_im + first_im * pred_re
        residual += [resid_re, resid_im]
        lead.append(
            (-(resid_re * cross_re - resid_im * cross_im), -(resid_re * cross_im + resid_im * cross_re))
        )
        trail.append(
            (-(resid_re * along_re + resid_im * along_im), -(resid_re * along_im - resid_im * along_re))
        )
    leading = [lead[2 * f][r] + lead[2 * f + 1][r] for f in range(2) for r in range(2)]
    trailing = [trail[f][r] + trail[f + 2][r] for f in range(2) for r in range(2)]
    return residual, leading, trailing


def nt_dot(left, right, **kw):
    return lax.dot_general(
        left, right, (((1,), (1,)), ((), ())), preferred_element_type=jnp.float32, **kw
    )


def chirped_rows(taper, chirp_ref):
    wide = taper.astype(jnp.float32)
    return jnp.concatenate(
        [
            taper,
            (wide * chirp_ref[0:1, :]).astype(jnp.bfloat16),
            (wide * chirp_ref[1:2, :]).astype(jnp.bfloat16),
        ],
        axis=0,
    )


def predict_kernel(
    sizes,
    contrib_ref,
    lead_ref,
    trail_ref,
    depth_ref,
    observed_ref,
    gains_ref,
    idents_ref,
    table_re_ref,
    table_im_ref,
    second_ref,
    third_ref,
    chirp_ref,
    residual_ref,
    grad_ref,
    got,
    lines,
    tapers,
    right,
    left,
    part_out,
    part_in,
    observed_in,
    record_out,
    record_in,
    got_send,
    got_recv,
    taper_send,
    taper_recv,
    observed_send,
    observed_recv,
    part_send,
    part_recv,
    record_send,
    record_recv,
):
    subgrids, pols, owners = sizes
    z, p, t = lax.axis_index("facet"), lax.axis_index("pol"), lax.axis_index("tm")
    slots = lead_ref.shape[0]
    _, groups, rows, width = contrib_ref.shape
    mesh_id = pl.DeviceIdType.MESH

    def remote(src, dst, send, recv, peer):
        return pltpu.make_async_remote_copy(
            src_ref=src,
            dst_ref=dst,
            send_sem=send,
            recv_sem=recv,
            device_id=peer,
            device_id_type=mesh_id,
        )

    across_total = subgrids * owners
    plane_total = pols * owners
    across = z * owners + t
    plane = p * owners + t

    def across_peer(d):
        other = lax.rem(across + d, across_total)
        return other, (other // owners, p, lax.rem(other, owners))

    def plane_peer(d):
        other = lax.rem(plane + d, plane_total)
        return other, (z, other // owners, lax.rem(other, owners))

    barrier = pltpu.get_barrier_semaphore()
    for d in range(1, across_total):
        pl.semaphore_signal(barrier, inc=1, device_id=across_peer(d)[1], device_id_type=mesh_id)
    for d in range(1, pols):
        q = lax.rem(p + d, pols)
        for o in range(owners):
            pl.semaphore_signal(barrier, inc=1, device_id=(z, q, o), device_id_type=mesh_id)
    pl.semaphore_wait(barrier, across_total - 1 + (pols - 1) * owners)

    copies = []
    for d in range(1, subgrids):
        other = lax.rem(z + d, subgrids)
        copies.append(
            remote(contrib_ref.at[other], got.at[z], got_send.at[d], got_recv.at[d], (other, p, t))
        )
    partner = lax.rem(t + 1, owners)
    taper_copies = [
        remote(ref, tapers.at[t, k], taper_send.at[k], taper_recv.at[k], (z, p, partner))
        for k, ref in enumerate((trail_ref, lead_ref))
    ]
    observed_copies = []
    for d in range(1, pols):
        q = lax.rem(p + d, pols)
        observed_copies.append(
            remote(
                observed_ref, observed_in.at[p], observed_send.at[d], observed_recv.at[d], (z, q, t)
            )
        )
    for copy in copies + taper_copies + observed_copies:
        copy.start()

    table_re = jnp.concatenate([table_re_ref[i, t] for i in range(FGRID)], axis=0)
    table_im = jnp.concatenate([table_im_ref[i, t] for i in range(FGRID)], axis=0)

    def prepare(owner, trail, lead):
        trail3 = chirped_rows(trail, chirp_ref)
        a = jnp.dot(trail3, second_ref[...], preferred_element_type=jnp.float32)
        b = jnp.dot(trail3, third_ref[...], preferred_element_type=jnp.float32)
        n0, n1, n2 = slice(0, slots), slice(slots, 2 * slots), slice(2 * slots, 3 * slots)
        right[owner, 0:slots, :] = a[n0].astype(jnp.bfloat16)
        right[owner, slots : 2 * slots, :] = (a[n1] - b[n2]).astype(jnp.bfloat16)
        right[owner, 2 * slots : 3 * slots, :] = b[n0].astype(jnp.bfloat16)
        right[owner, 3 * slots : 4 * slots, :] = (b[n1] + a[n2]).astype(jnp.bfloat16)
        lead3 = chirped_rows(lead, chirp_ref)
        u = nt_dot(table_re, lead3)
        v = nt_dot(table_im, lead3)
        left[owner, 0] = u[:, n0]
        left[owner, 1] = v[:, n0]
        left[owner, 2] = u[:, n1] - v[:, n2]
        left[owner, 3] = u[:, n2] + v[:, n1]

    prepare(t, trail_ref[...], lead_ref[...])
    got[z] = contrib_ref[z]
    for copy in taper_copies:
        copy.wait()
    prepare(partner, tapers[partner, 0], tapers[partner, 1])
    for copy in copies:
        copy.wait()
    if width == 2 * SG:
        whole = got[...].reshape(subgrids * groups * rows, width)
    else:
        for f in range(subgrids * groups):
            i, j = f // FGRID, f % FGRID
            lines[i * rows : (i + 1) * rows, j * 2 * MC : (j + 1) * 2 * MC] = got[
                f // groups, f % groups
            ]
        whole = lines[...]
    for o in range(owners):
        spread = nt_dot(whole, right[o])
        for w in range(NW):
            g_re = spread[:, w * slots : (w + 1) * slots]
            g_im = spread[:, (NW + w) * slots : (NW + w + 1) * slots]
            l_re, l_im = left[o, 2 * w], left[o, 2 * w + 1]
            part_out[o, 2 * w : 2 * w + 1, :] = jnp.sum(l_re * g_re - l_im * g_im, axis=0, keepdims=True)
            part_out[o, 2 * w + 1 : 2 * w + 2, :] = jnp.sum(
                l_re * g_im + l_im * g_re, axis=0, keepdims=True
            )
        part_out[o, 2 * NW :, :] = jnp.zeros((8 - 2 * NW, slots), jnp.float32)

    part_copies = []
    for d in range(1, plane_total):
        other, peer = plane_peer(d)
        part_copies.append(
            remote(
                part_out.at[lax.rem(other, owners)],
                part_in.at[plane],
                part_send.at[d],
                part_recv.at[d],
                peer,
            )
        )
    for copy in part_copies:
        copy.start()
    part_in[plane] = part_out[t]
    observed_in[p] = observed_ref[...]
    for copy in observed_copies:
        copy.wait()
    observed = observed_in[0]
    for q in range(1, pols):
        observed = observed + observed_in[q]
    depth = depth_ref[...].astype(jnp.float32)
    for copy in part_copies:
        copy.wait()

    pred = []
    per_pol = part_in.shape[0] // NPOL
    for q in range(NPOL):
        block = part_in[q * per_pol]
        for o in range(1, per_pol):
            block = block + part_in[q * per_pol + o]
        pred.append(
            tuple(
                sum(depth[w : w + 1] * block[2 * w + c : 2 * w + c + 1] for w in range(NW))
                for c in range(2)
            )
        )
    gains = gains_ref[...]
    idents = idents_ref[...]
    residual, leading, trailing = model_terms(
        pred,
        [observed[k : k + 1] for k in range(2 * NPOL)],
        [gains[k : k + 1] for k in range(4)],
        [gains[4 + k : 5 + k] for k in range(4)],
        idents[3:4],
    )
    for k in range(3):
        record_out[k : k + 1, :] = idents[k : k + 1]
    for k in range(4):
        record_out[3 + k : 4 + k, :] = leading[k]
        record_out[7 + k : 8 + k, :] = trailing[k]
    record_out[11:, :] = jnp.zeros((5, slots), jnp.float32)
    record_copies = []
    for d in range(1, across_total):
        other, peer = across_peer(d)
        record_copies.append(
            remote(record_out, record_in.at[across], record_send.at[d], record_recv.at[d], peer)
        )
    for copy in record_copies:
        copy.start()
    record_in[across] = record_out[...]
    for k in range(2 * NPOL):
        residual_ref[k : k + 1, :] = residual[k]
    for copy in record_copies:
        copy.wait()

    piece = jnp.concatenate([record_in[d] for d in range(across_total)], axis=1)
    own_count = grad_ref.shape[1]
    index = (z * pols + p) * owners + t
    mine = (index * own_count + lax.broadcasted_iota(jnp.int32, (own_count, 1), 0)).astype(
        jnp.float32
    )
    match_first = mine == piece[0:1]
    match_second = mine == piece[1:2]
    weighted = jnp.concatenate(
        [
            jnp.where(match_first, piece[3 + k : 4 + k], 0.0)
            + jnp.where(match_second, piece[7 + k : 8 + k], 0.0)
            for k in range(4)
        ],
        axis=0,
    )
    high = weighted.astype(jnp.bfloat16)
    low = (weighted - high.astype(jnp.float32)).astype(jnp.bfloat16)
    channel_ids = lax.broadcasted_iota(jnp.int32, (NCH, 1), 0).astype(jnp.float32)
    onehot = jnp.where(channel_ids == piece[2:3], 1.0, 0.0).astype(jnp.bfloat16)
    summed = nt_dot(high, onehot) + nt_dot(low, onehot)
    for k in range(4):
        grad_ref[k] = grad_scale * summed[k * own_count : (k + 1) * own_count]


def predict(sizes, own_count, *operands):
    subgrids, pols, owners = sizes
    contrib, lead = operands[0], operands[1]
    _, groups, rows, width = contrib.shape
    slots = lead.shape[0]
    vmem = pl.BlockSpec(memory_space=pltpu.VMEM)
    dma = lambda n: pltpu.SemaphoreType.DMA((n,))
    across_total, plane_total = subgrids * owners, pols * owners
    return pl.pallas_call(
        functools.partial(predict_kernel, sizes),
        out_shape=(
            jax.ShapeDtypeStruct((2 * NPOL, slots), jnp.float32),
            jax.ShapeDtypeStruct((4, own_count, NCH), jnp.float32),
        ),
        in_specs=[vmem] * len(operands),
        out_specs=(vmem, vmem),
        scratch_shapes=[
            pltpu.VMEM(contrib.shape, jnp.bfloat16),
            pltpu.VMEM((FGRID * rows, 2 * SG), jnp.bfloat16),
            pltpu.VMEM((owners, 2, slots, SG), jnp.bfloat16),
            pltpu.VMEM((owners, 2 * NW * slots, 2 * SG), jnp.bfloat16),
            pltpu.VMEM((owners, 4, FGRID * rows, slots), jnp.float32),
            pltpu.VMEM((owners, 8, slots), jnp.float32),
            pltpu.VMEM((plane_total, 8, slots), jnp.float32),
            pltpu.VMEM((pols, 8, slots), jnp.float32),
            pltpu.VMEM((16, slots), jnp.float32),
            pltpu.VMEM((across_total, 16, slots), jnp.float32),
            dma(subgrids),
            dma(subgrids),
            dma(2),
            dma(2),
            dma(pols),
            dma(pols),
            dma(plane_total),
            dma(plane_total),
            dma(across_total),
            dma(across_total),
        ],
        compiler_params=pltpu.CompilerParams(
            collective_id=0, has_side_effects=True, vmem_limit_bytes=48 << 20
        ),
    )(*operands)


def on_device(
    tile_spectral_lines,
    taper_leading_axis,
    taper_trailing_axis,
    depth_layer_factors,
    measured_correlations,
    visibility_groups_table,
    antenna_links,
    complex_receiver_factors,
):
    sizes = tuple(lax.axis_size(name) for name in ("facet", "pol", "tm"))
    subgrids, pols, owners = sizes
    slots = taper_leading_axis.shape[2]
    quarter = measured_correlations.shape[3]
    rows = tile_spectral_lines.shape[3]
    pol_index = lax.axis_index("pol")

    block_table = visibility_groups_table.reshape(3, visibility_groups_table.shape[3])
    observed = measured_correlations.reshape(2 * NPOL, quarter)
    in_quarter = (jnp.arange(slots, dtype=jnp.int32) // quarter == pol_index)[None, :]
    observed = jnp.where(in_quarter, jnp.tile(observed, (1, pols)), 0.0)

    contrib, gains, idents = fourier(
        tile_spectral_lines[:, 0],
        subgrids,
        slots,
        block_table,
        antenna_links,
        complex_receiver_factors,
    )
    table_re, table_im, second, third = [jnp.asarray(t) for t in subgrid_tables()]
    cosine, sine = chirp_line()
    own_count = NST // (subgrids * pols * owners)
    residual, grad = predict(
        sizes,
        own_count,
        contrib,
        taper_leading_axis.reshape(slots, SG),
        taper_trailing_axis.reshape(slots, SG),
        depth_layer_factors.reshape(NW, slots),
        observed,
        gains,
        idents,
        table_re.reshape(FGRID, owners, rows, SG),
        table_im.reshape(FGRID, owners, rows, SG),
        second,
        third,
        jnp.asarray(np.stack([cosine, sine])),
    )
    residual = lax.dynamic_slice_in_dim(residual, pol_index * quarter, quarter, 1)
    gain_grad = jnp.transpose(grad, (1, 2, 0)).reshape(own_count, 4 * NCH)
    return residual.reshape(1, 2 * NPOL, 1, quarter), gain_grad


def solution(mesh):
    return jax.shard_map(
        on_device,
        mesh=mesh,
        in_specs=(
            P("facet", "pol", None, "tm", None),
            P("facet", "tm", None, None),
            P("facet", "tm", None, None),
            P("facet", "tm", None, None),
            P("facet", None, "tm", "pol"),
            P("facet", "tm", None, None),
            P(),
            P(),
        ),
        out_specs=(P("facet", None, "tm", "pol"), P(("facet", "pol", "tm"), None)),
        check_vma=False,
    )
```

```python
import functools
import math

import jax
import jax.numpy as jnp
import numpy as np
from jax import lax
from jax.experimental import pallas as pl
from jax.experimental.pallas import tpu as pltpu
from jax.sharding import PartitionSpec as P

FGRID = 8
FS = 4096
MC = 64
SG = 512
NPOL = 4
NW = 2
NCH = 256
NST = 512
CHUNK = 512

w_chirp = 0.37
grad_scale = 0.1


def unit_angles(left, right, length):
    product = np.outer(np.arange(left), np.arange(right)) % length
    return 2.0 * math.pi * product / length


def fourier_factors(subgrids):
    spread = FS // MC
    alpha = unit_angles(FS // spread, MC, MC)
    p = np.concatenate([np.cos(alpha), -np.sin(alpha)], axis=1) / math.sqrt(FS)
    q = np.concatenate([-np.sin(alpha), -np.cos(alpha)], axis=1) / math.sqrt(FS)
    beta = unit_angles(spread, subgrids * MC, FS).reshape(spread, subgrids, 1, MC)
    beta = np.broadcast_to(beta, (spread, subgrids, 2, MC)).reshape(spread, subgrids * 2 * MC)
    tile = lambda t: np.tile(t, (1, subgrids)).astype(np.float32)
    return (
        tile(p),
        tile(q),
        np.cos(beta).astype(np.float32),
        np.sin(beta).astype(np.float32),
    )


def fetch_lookups(block_ref, links_ref, gain_ref, window, channel_gain, window_sem, gain_sem):
    blocks, _, span = window.shape
    copies = []
    for b in range(blocks):
        first = jnp.minimum(block_ref[1, b] // 128 * 128, links_ref.shape[1] - span)
        first = pl.multiple_of(first, 128)
        copies.append(
            pltpu.make_async_copy(
                links_ref.at[:, pl.ds(first, span)], window.at[b], window_sem.at[b]
            )
        )
        copies.append(
            pltpu.make_async_copy(
                gain_ref.at[block_ref[0, b]], channel_gain.at[b], gain_sem.at[b]
            )
        )
    return copies


def use_lookups(block_ref, links_ref, window, channel_gain, gains_ref, idents_ref):
    blocks, _, span = window.shape
    slots = idents_ref.shape[1]
    lane = lax.broadcasted_iota(jnp.int32, (1, slots), 1)
    place = lax.broadcasted_iota(jnp.int32, (span, slots), 0)
    lane_tall = lax.broadcasted_iota(jnp.int32, (span, slots), 1)
    begin = jnp.int32(0)
    member, picks = [], []
    channel = jnp.zeros((1, slots), jnp.float32)
    alive = jnp.zeros((1, slots), jnp.float32)
    for b in range(blocks):
        offset, amount = block_ref[1, b], block_ref[2, b]
        first = jnp.minimum(offset // 128 * 128, links_ref.shape[1] - span)
        inside = jnp.where((lane >= begin) & (lane < begin + amount), 1.0, 0.0)
        member.append(inside)
        alive += inside
        channel += inside * block_ref[0, b].astype(jnp.float32)
        hit = place == lane_tall + (offset - first - begin)
        picks.append((jnp.where(hit, 1.0, 0.0) * inside).astype(jnp.bfloat16))
        begin = begin + amount
    links = jnp.concatenate([window[b] for b in range(blocks)], axis=1)
    upper = links // 16
    lower = links - 16 * upper
    pieces = jnp.concatenate([upper, lower], axis=0).astype(jnp.float32).astype(jnp.bfloat16)
    found = jnp.dot(
        pieces, jnp.concatenate(picks, axis=0), preferred_element_type=jnp.float32
    )
    stations = 16.0 * found[0:2] + found[2:4]
    table = channel_gain[...].reshape(blocks * 4, channel_gain.shape[2])
    high = table.astype(jnp.bfloat16)
    rest = table - high.astype(jnp.float32)
    middle = rest.astype(jnp.bfloat16)
    low = (rest - middle.astype(jnp.float32)).astype(jnp.bfloat16)
    names = lax.broadcasted_iota(jnp.int32, (table.shape[1], 1), 0).astype(jnp.float32)
    for side in range(2):
        pick = jnp.where(names == stations[side : side + 1], 1.0, 0.0).astype(jnp.bfloat16)
        rows = (
            jnp.dot(high, pick, preferred_element_type=jnp.float32)
            + jnp.dot(middle, pick, preferred_element_type=jnp.float32)
            + jnp.dot(low, pick, preferred_element_type=jnp.float32)
        )
        chosen = member[0] * rows[0:4]
        for b in range(1, blocks):
            chosen = chosen + member[b] * rows[4 * b : 4 * b + 4]
        gains_ref[4 * side : 4 * side + 4, :] = chosen
    idents_ref[0:2, :] = stations
    idents_ref[2:3, :] = channel
    idents_ref[3:4, :] = alive
    idents_ref[4:8, :] = jnp.zeros((4, slots), jnp.float32)


def fourier_kernel(
    block_ref,
    links_ref,
    gain_ref,
    p_ref,
    q_ref,
    c_ref,
    s_ref,
    x_ref,
    o_ref,
    gains_ref,
    idents_ref,
    table,
    total,
    window,
    channel_gain,
    window_sem,
    gain_sem,
):
    step = pl.program_id(0)
    copies = fetch_lookups(
        block_ref, links_ref, gain_ref, window, channel_gain, window_sem, gain_sem
    )

    @pl.when(step == 0)
    def _():
        for copy in copies:
            copy.start()

    @pl.when(step == pl.num_programs(0) - 1)
    def _():
        for copy in copies:
            copy.wait()
        use_lookups(block_ref, links_ref, window, channel_gain, gains_ref, idents_ref)

    facets, _, rows, chunk = x_ref.shape
    subgrids = o_ref.shape[0]
    spread = c_ref.shape[0]
    cosine, sine = c_ref[...], s_ref[...]
    for part in range(chunk // spread):
        lead = p_ref[part : part + 1, :]
        other = q_ref[part : part + 1, :]
        table[part * spread : (part + 1) * spread, :] = (lead * cosine + other * sine).astype(
            jnp.bfloat16
        )
    x = x_ref[...].reshape(facets * 2 * rows, chunk)
    product = jnp.dot(x, table[...], preferred_element_type=jnp.float32)

    @pl.when(step == 0)
    def _():
        total[...] = product

    @pl.when(step > 0)
    def _():
        total[...] += product

    @pl.when(step == pl.num_programs(0) - 1)
    def _():
        lane = lax.broadcasted_iota(jnp.int32, (rows, 2 * MC), 1)
        sign = jnp.where(lane < MC, -1.0, 1.0)
        packed = o_ref.shape[3] // (2 * MC)
        for f in range(facets):
            for s in range(subgrids):
                cut = slice(s * 2 * MC, (s + 1) * 2 * MC)
                first = total[2 * f * rows : (2 * f + 1) * rows, cut]
                second = total[(2 * f + 1) * rows : (2 * f + 2) * rows, cut]
                value = first + sign * pltpu.roll(second, MC, 1)
                j = f % packed
                o_ref[s, f // packed, :, j * 2 * MC : (j + 1) * 2 * MC] = value.astype(jnp.bfloat16)


def fourier(x, subgrids, slots, block_table, links, station_gains):
    facets, _, rows, length = x.shape
    width = subgrids * 2 * MC
    spread = FS // MC
    packed = FGRID if facets % FGRID == 0 else 1
    per_step = CHUNK // spread
    blocks = block_table.shape[1]
    span = slots + 128
    in_place = lambda array: pltpu.with_memory_space_constraint(array, pltpu.HBM)
    factors = [in_place(jnp.asarray(t)) for t in fourier_factors(subgrids)]
    out = (subgrids, facets // packed, rows, packed * 2 * MC)
    return pl.pallas_call(
        fourier_kernel,
        out_shape=(
            jax.ShapeDtypeStruct(out, jnp.bfloat16),
            jax.ShapeDtypeStruct((8, slots), jnp.float32),
            jax.ShapeDtypeStruct((8, slots), jnp.float32),
        ),
        grid=(length // CHUNK,),
        in_specs=[
            pl.BlockSpec(memory_space=pltpu.SMEM),
            pl.BlockSpec(memory_space=pltpu.HBM),
            pl.BlockSpec(memory_space=pltpu.HBM),
            pl.BlockSpec((per_step, width), lambda g: (g, 0)),
            pl.BlockSpec((per_step, width), lambda g: (g, 0)),
            pl.BlockSpec((spread, width), lambda g: (0, 0)),
            pl.BlockSpec((spread, width), lambda g: (0, 0)),
            pl.BlockSpec((facets, 2, rows, CHUNK), lambda g: (0, 0, 0, g)),
        ],
        out_specs=(
            pl.BlockSpec(out, lambda g: (0, 0, 0, 0)),
            pl.BlockSpec((8, slots), lambda g: (0, 0)),
            pl.BlockSpec((8, slots), lambda g: (0, 0)),
        ),
        scratch_shapes=[
            pltpu.VMEM((CHUNK, width), jnp.bfloat16),
            pltpu.VMEM((facets * 2 * rows, width), jnp.float32),
            pltpu.VMEM((blocks, 2, span), jnp.int32),
            pltpu.VMEM((blocks, 4, NST), jnp.float32),
            pltpu.SemaphoreType.DMA((blocks,)),
            pltpu.SemaphoreType.DMA((blocks,)),
        ],
        compiler_params=pltpu.CompilerParams(
            dimension_semantics=("arbitrary",), vmem_limit_bytes=48 << 20
        ),
    )(
        block_table,
        in_place(links),
        in_place(station_gains),
        *factors,
        x,
    )


def subgrid_tables():
    angle = unit_angles(SG, SG, SG)
    re = np.cos(angle) / math.sqrt(SG)
    im = np.sin(angle) / math.sqrt(SG)
    blocks = lambda t: t.reshape(SG, FGRID, MC)
    second = np.stack([blocks(re), -blocks(im)], axis=2).reshape(SG, 2 * SG)
    return [t.astype(jnp.bfloat16) for t in (re, im, second)]


def chirp_line():
    offset = np.arange(SG) - SG // 2
    angle = 2.0 * math.pi * w_chirp * (offset * offset) / float(SG * SG)
    return np.cos(angle).astype(np.float32), np.sin(angle).astype(np.float32)


def model_terms(pred, observed, first, second, alive):
    residual, lead, trail = [], [], []
    for p in range(NPOL):
        f1, f2 = p // 2, p % 2
        pred_re, pred_im = pred[p]
        first_re, first_im = first[2 * f1], first[2 * f1 + 1]
        second_re, second_im = second[2 * f2], second[2 * f2 + 1]
        both_re = first_re * second_re + first_im * second_im
        both_im = first_im * second_re - first_re * second_im
        resid_re = alive * (observed[2 * p] - (both_re * pred_re - both_im * pred_im))
        resid_im = alive * (observed[2 * p + 1] - (both_re * pred_im + both_im * pred_re))
        cross_re = second_re * pred_re + second_im * pred_im
        cross_im = second_im * pred_re - second_re * pred_im
        along_re = first_re * pred_re - first_im * pred_im
        along_im = first_re * pred_im + first_im * pred_re
        residual += [resid_re, resid_im]
        lead.append(
            (-(resid_re * cross_re - resid_im * cross_im), -(resid_re * cross_im + resid_im * cross_re))
        )
        trail.append(
            (-(resid_re * along_re + resid_im * along_im), -(resid_re * along_im - resid_im * along_re))
        )
    leading = [lead[2 * f][r] + lead[2 * f + 1][r] for f in range(2) for r in range(2)]
    trailing = [trail[f][r] + trail[f + 2][r] for f in range(2) for r in range(2)]
    return residual, leading, trailing


def nt_dot(left, right, **kw):
    return lax.dot_general(
        left, right, (((1,), (1,)), ((), ())), preferred_element_type=jnp.float32, **kw
    )


def chirped_rows(taper, chirp_ref):
    wide = taper.astype(jnp.float32)
    return jnp.concatenate(
        [
            taper,
            (wide * chirp_ref[0:1, :]).astype(jnp.bfloat16),
            (wide * chirp_ref[1:2, :]).astype(jnp.bfloat16),
        ],
        axis=0,
    )


def predict_kernel(
    sizes,
    contrib_ref,
    lead_ref,
    trail_ref,
    depth_ref,
    observed_ref,
    gains_ref,
    idents_ref,
    table_re_ref,
    table_im_ref,
    second_ref,
    chirp_ref,
    residual_ref,
    grad_ref,
    got,
    lines,
    tapers,
    right,
    left,
    part_out,
    part_in,
    observed_out,
    observed_in,
    record_out,
    record_in,
    got_send,
    got_recv,
    taper_send,
    taper_recv,
    observed_send,
    observed_recv,
    part_send,
    part_recv,
    record_send,
    record_recv,
):
    subgrids, pols, owners = sizes
    z, p, t = lax.axis_index("facet"), lax.axis_index("pol"), lax.axis_index("tm")
    slots = lead_ref.shape[0]
    _, groups, rows, width = contrib_ref.shape
    mesh_id = pl.DeviceIdType.MESH

    def remote(src, dst, send, recv, peer):
        return pltpu.make_async_remote_copy(
            src_ref=src,
            dst_ref=dst,
            send_sem=send,
            recv_sem=recv,
            device_id=peer,
            device_id_type=mesh_id,
        )

    across_total = subgrids * owners
    plane_total = pols * owners
    across = z * owners + t
    plane = p * owners + t

    def across_peer(d):
        other = lax.rem(across + d, across_total)
        return other, (other // owners, p, lax.rem(other, owners))

    def plane_peer(d):
        other = lax.rem(plane + d, plane_total)
        return other, (z, other // owners, lax.rem(other, owners))

    barrier = pltpu.get_barrier_semaphore()
    for d in range(1, across_total):
        pl.semaphore_signal(barrier, inc=1, device_id=across_peer(d)[1], device_id_type=mesh_id)
    for d in range(1, pols):
        q = lax.rem(p + d, pols)
        for o in range(owners):
            pl.semaphore_signal(barrier, inc=1, device_id=(z, q, o), device_id_type=mesh_id)
    pl.semaphore_wait(barrier, across_total - 1 + (pols - 1) * owners)

    quarter = observed_ref.shape[1]
    place = lax.broadcasted_iota(jnp.int32, (2 * NPOL, slots), 1)
    observed_out[...] = jnp.where(
        (place >= p * quarter) & (place < (p + 1) * quarter),
        jnp.concatenate([observed_ref[...]] * pols, axis=1),
        0.0,
    )
    copies = []
    for d in range(1, subgrids):
        other = lax.rem(z + d, subgrids)
        copies.append(
            remote(contrib_ref.at[other], got.at[z], got_send.at[d], got_recv.at[d], (other, p, t))
        )
    partner = lax.rem(t + 1, owners)
    taper_copies = [
        remote(ref, tapers.at[t, k], taper_send.at[k], taper_recv.at[k], (z, p, partner))
        for k, ref in enumerate((trail_ref, lead_ref))
    ]
    observed_copies = []
    for d in range(1, pols):
        q = lax.rem(p + d, pols)
        observed_copies.append(
            remote(
                observed_out, observed_in.at[p], observed_send.at[d], observed_recv.at[d], (z, q, t)
            )
        )
    for copy in copies + taper_copies + observed_copies:
        copy.start()

    table_re = jnp.concatenate([table_re_ref[i, t] for i in range(FGRID)], axis=0)
    table_im = jnp.concatenate([table_im_ref[i, t] for i in range(FGRID)], axis=0)

    turn = jnp.where(
        lax.broadcasted_iota(jnp.int32, (3 * slots, 2 * MC), 1) < MC, -1.0, 1.0
    )

    def prepare(owner, trail, lead):
        trail3 = chirped_rows(trail, chirp_ref)
        a = jnp.dot(trail3, second_ref[...], preferred_element_type=jnp.float32)
        b = jnp.concatenate(
            [
                turn * pltpu.roll(a[:, j * 2 * MC : (j + 1) * 2 * MC], MC, 1)
                for j in range(a.shape[1] // (2 * MC))
            ],
            axis=1,
        )
        n0, n1, n2 = slice(0, slots), slice(slots, 2 * slots), slice(2 * slots, 3 * slots)
        right[owner, 0:slots, :] = a[n0].astype(jnp.bfloat16)
        right[owner, slots : 2 * slots, :] = (a[n1] - b[n2]).astype(jnp.bfloat16)
        right[owner, 2 * slots : 3 * slots, :] = b[n0].astype(jnp.bfloat16)
        right[owner, 3 * slots : 4 * slots, :] = (b[n1] + a[n2]).astype(jnp.bfloat16)
        lead3 = chirped_rows(lead, chirp_ref)
        u = nt_dot(table_re, lead3)
        v = nt_dot(table_im, lead3)
        left[owner, 0] = u[:, n0]
        left[owner, 1] = v[:, n0]
        left[owner, 2] = u[:, n1] - v[:, n2]
        left[owner, 3] = u[:, n2] + v[:, n1]

    prepare(t, trail_ref[...], lead_ref[...])
    got[z] = contrib_ref[z]
    for copy in taper_copies:
        copy.wait()
    prepare(partner, tapers[partner, 0], tapers[partner, 1])
    for copy in copies:
        copy.wait()
    if width == 2 * SG:
        whole = got[...].reshape(subgrids * groups * rows, width)
    else:
        for f in range(subgrids * groups):
            i, j = f // FGRID, f % FGRID
            lines[i * rows : (i + 1) * rows, j * 2 * MC : (j + 1) * 2 * MC] = got[
                f // groups, f % groups
            ]
        whole = lines[...]
    for o in range(owners):
        spread = nt_dot(whole, right[o])
        for w in range(NW):
            g_re = spread[:, w * slots : (w + 1) * slots]
            g_im = spread[:, (NW + w) * slots : (NW + w + 1) * slots]
            l_re, l_im = left[o, 2 * w], left[o, 2 * w + 1]
            part_out[o, 2 * w : 2 * w + 1, :] = jnp.sum(l_re * g_re - l_im * g_im, axis=0, keepdims=True)
            part_out[o, 2 * w + 1 : 2 * w + 2, :] = jnp.sum(
                l_re * g_im + l_im * g_re, axis=0, keepdims=True
            )
        part_out[o, 2 * NW :, :] = jnp.zeros((8 - 2 * NW, slots), jnp.float32)

    part_copies = []
    for d in range(1, plane_total):
        other, peer = plane_peer(d)
        part_copies.append(
            remote(
                part_out.at[lax.rem(other, owners)],
                part_in.at[plane],
                part_send.at[d],
                part_recv.at[d],
                peer,
            )
        )
    for copy in part_copies:
        copy.start()
    part_in[plane] = part_out[t]
    observed_in[p] = observed_out[...]
    for copy in observed_copies:
        copy.wait()
    observed = observed_in[0]
    for q in range(1, pols):
        observed = observed + observed_in[q]
    depth = depth_ref[...].astype(jnp.float32)
    for copy in part_copies:
        copy.wait()

    pred = []
    per_pol = part_in.shape[0] // NPOL
    for q in range(NPOL):
        block = part_in[q * per_pol]
        for o in range(1, per_pol):
            block = block + part_in[q * per_pol + o]
        pred.append(
            tuple(
                sum(depth[w : w + 1] * block[2 * w + c : 2 * w + c + 1] for w in range(NW))
                for c in range(2)
            )
        )
    gains = gains_ref[...]
    idents = idents_ref[...]
    residual, leading, trailing = model_terms(
        pred,
        [observed[k : k + 1] for k in range(2 * NPOL)],
        [gains[k : k + 1] for k in range(4)],
        [gains[4 + k : 5 + k] for k in range(4)],
        idents[3:4],
    )
    for k in range(3):
        record_out[k : k + 1, :] = idents[k : k + 1]
    for k in range(4):
        record_out[3 + k : 4 + k, :] = leading[k]
        record_out[7 + k : 8 + k, :] = trailing[k]
    record_out[11:, :] = jnp.zeros((5, slots), jnp.float32)
    record_copies = []
    for d in range(1, across_total):
        other, peer = across_peer(d)
        record_copies.append(
            remote(record_out, record_in.at[across], record_send.at[d], record_recv.at[d], peer)
        )
    for copy in record_copies:
        copy.start()
    record_in[across] = record_out[...]
    rest = jnp.concatenate(residual, axis=0)
    own_rest = jnp.zeros((2 * NPOL, quarter), jnp.float32)
    for q in range(pols):
        own_rest = jnp.where(p == q, rest[:, q * quarter : (q + 1) * quarter], own_rest)
    residual_ref[...] = own_rest
    for copy in record_copies:
        copy.wait()

    piece = jnp.concatenate([record_in[d] for d in range(across_total)], axis=1)
    own_count = grad_ref.shape[1]
    index = (z * pols + p) * owners + t
    mine = (index * own_count + lax.broadcasted_iota(jnp.int32, (own_count, 1), 0)).astype(
        jnp.float32
    )
    match_first = mine == piece[0:1]
    match_second = mine == piece[1:2]
    weighted = jnp.concatenate(
        [
            jnp.where(match_first, piece[3 + k : 4 + k], 0.0)
            + jnp.where(match_second, piece[7 + k : 8 + k], 0.0)
            for k in range(4)
        ],
        axis=0,
    )
    high = weighted.astype(jnp.bfloat16)
    low = (weighted - high.astype(jnp.float32)).astype(jnp.bfloat16)
    channel_ids = lax.broadcasted_iota(jnp.int32, (NCH, 1), 0).astype(jnp.float32)
    onehot = jnp.where(channel_ids == piece[2:3], 1.0, 0.0).astype(jnp.bfloat16)
    summed = nt_dot(high, onehot) + nt_dot(low, onehot)
    for k in range(4):
        grad_ref[k] = grad_scale * summed[k * own_count : (k + 1) * own_count]


def predict(sizes, own_count, *operands):
    subgrids, pols, owners = sizes
    contrib, lead = operands[0], operands[1]
    _, groups, rows, width = contrib.shape
    slots = lead.shape[0]
    vmem = pl.BlockSpec(memory_space=pltpu.VMEM)
    dma = lambda n: pltpu.SemaphoreType.DMA((n,))
    across_total, plane_total = subgrids * owners, pols * owners
    return pl.pallas_call(
        functools.partial(predict_kernel, sizes),
        out_shape=(
            jax.ShapeDtypeStruct((2 * NPOL, slots // pols), jnp.float32),
            jax.ShapeDtypeStruct((4, own_count, NCH), jnp.float32),
        ),
        in_specs=[vmem] * len(operands),
        out_specs=(vmem, vmem),
        scratch_shapes=[
            pltpu.VMEM(contrib.shape, jnp.bfloat16),
            pltpu.VMEM((FGRID * rows, 2 * SG), jnp.bfloat16),
            pltpu.VMEM((owners, 2, slots, SG), jnp.bfloat16),
            pltpu.VMEM((owners, 2 * NW * slots, 2 * SG), jnp.bfloat16),
            pltpu.VMEM((owners, 4, FGRID * rows, slots), jnp.float32),
            pltpu.VMEM((owners, 8, slots), jnp.float32),
            pltpu.VMEM((plane_total, 8, slots), jnp.float32),
            pltpu.VMEM((8, slots), jnp.float32),
            pltpu.VMEM((pols, 8, slots), jnp.float32),
            pltpu.VMEM((16, slots), jnp.float32),
            pltpu.VMEM((across_total, 16, slots), jnp.float32),
            dma(subgrids),
            dma(subgrids),
            dma(2),
            dma(2),
            dma(pols),
            dma(pols),
            dma(plane_total),
            dma(plane_total),
            dma(across_total),
            dma(across_total),
        ],
        compiler_params=pltpu.CompilerParams(
            collective_id=0, has_side_effects=True, vmem_limit_bytes=48 << 20
        ),
    )(*operands)


def on_device(
    tile_spectral_lines,
    taper_leading_axis,
    taper_trailing_axis,
    depth_layer_factors,
    measured_correlations,
    visibility_groups_table,
    antenna_links,
    complex_receiver_factors,
):
    sizes = tuple(lax.axis_size(name) for name in ("facet", "pol", "tm"))
    subgrids, pols, owners = sizes
    slots = taper_leading_axis.shape[2]
    quarter = measured_correlations.shape[3]
    rows = tile_spectral_lines.shape[3]

    block_table = visibility_groups_table.reshape(3, visibility_groups_table.shape[3])
    observed = measured_correlations.reshape(2 * NPOL, quarter)

    contrib, gains, idents = fourier(
        tile_spectral_lines[:, 0],
        subgrids,
        slots,
        block_table,
        antenna_links,
        complex_receiver_factors,
    )
    table_re, table_im, second = [jnp.asarray(t) for t in subgrid_tables()]
    cosine, sine = chirp_line()
    own_count = NST // (subgrids * pols * owners)
    residual, grad = predict(
        sizes,
        own_count,
        contrib,
        taper_leading_axis.reshape(slots, SG),
        taper_trailing_axis.reshape(slots, SG),
        depth_layer_factors.reshape(NW, slots),
        observed,
        gains,
        idents,
        table_re.reshape(FGRID, owners, rows, SG),
        table_im.reshape(FGRID, owners, rows, SG),
        second,
        jnp.asarray(np.stack([cosine, sine])),
    )
    gain_grad = jnp.transpose(grad, (1, 2, 0)).reshape(own_count, 4 * NCH)
    return residual.reshape(1, 2 * NPOL, 1, quarter), gain_grad


def solution(mesh):
    return jax.shard_map(
        on_device,
        mesh=mesh,
        in_specs=(
            P("facet", "pol", None, "tm", None),
            P("facet", "tm", None, None),
            P("facet", "tm", None, None),
            P("facet", "tm", None, None),
            P("facet", None, "tm", "pol"),
            P("facet", "tm", None, None),
            P(),
            P(),
        ),
        out_specs=(P("facet", None, "tm", "pol"), P(("facet", "pol", "tm"), None)),
        check_vma=False,
    )
```

```python
import functools
import math

import jax
import jax.numpy as jnp
import numpy as np
from jax import lax
from jax.experimental import pallas as pl
from jax.experimental.pallas import tpu as pltpu
from jax.sharding import PartitionSpec as P

FGRID = 8
FS = 4096
MC = 64
SG = 512
NPOL = 4
NW = 2
NCH = 256
NST = 512
CHUNK = 1024

w_chirp = 0.37
grad_scale = 0.1


def unit_angles(left, right, length):
    product = np.outer(np.arange(left), np.arange(right)) % length
    return 2.0 * math.pi * product / length


def fourier_factors(subgrids):
    spread = FS // MC
    alpha = unit_angles(FS // spread, MC, MC)
    p = np.concatenate([np.cos(alpha), -np.sin(alpha)], axis=1) / math.sqrt(FS)
    q = np.concatenate([-np.sin(alpha), -np.cos(alpha)], axis=1) / math.sqrt(FS)
    beta = unit_angles(spread, subgrids * MC, FS).reshape(spread, subgrids, 1, MC)
    beta = np.broadcast_to(beta, (spread, subgrids, 2, MC)).reshape(spread, subgrids * 2 * MC)
    tile = lambda t: np.tile(t, (1, subgrids)).astype(np.float32)
    return (
        tile(p),
        tile(q),
        np.cos(beta).astype(np.float32),
        np.sin(beta).astype(np.float32),
    )


def fetch_lookups(block_ref, links_ref, gain_ref, window, channel_gain, window_sem, gain_sem):
    blocks, _, span = window.shape
    copies = []
    for b in range(blocks):
        first = jnp.minimum(block_ref[1, b] // 128 * 128, links_ref.shape[1] - span)
        first = pl.multiple_of(first, 128)
        copies.append(
            pltpu.make_async_copy(
                links_ref.at[:, pl.ds(first, span)], window.at[b], window_sem.at[b]
            )
        )
        copies.append(
            pltpu.make_async_copy(
                gain_ref.at[block_ref[0, b]], channel_gain.at[b], gain_sem.at[b]
            )
        )
    return copies


def use_lookups(block_ref, links_ref, window, channel_gain, gains_ref, idents_ref):
    blocks, _, span = window.shape
    slots = idents_ref.shape[1]
    lane = lax.broadcasted_iota(jnp.int32, (1, slots), 1)
    place = lax.broadcasted_iota(jnp.int32, (span, slots), 0)
    lane_tall = lax.broadcasted_iota(jnp.int32, (span, slots), 1)
    begin = jnp.int32(0)
    member, picks = [], []
    channel = jnp.zeros((1, slots), jnp.float32)
    alive = jnp.zeros((1, slots), jnp.float32)
    for b in range(blocks):
        offset, amount = block_ref[1, b], block_ref[2, b]
        first = jnp.minimum(offset // 128 * 128, links_ref.shape[1] - span)
        inside = jnp.where((lane >= begin) & (lane < begin + amount), 1.0, 0.0)
        member.append(inside)
        alive += inside
        channel += inside * block_ref[0, b].astype(jnp.float32)
        hit = place == lane_tall + (offset - first - begin)
        picks.append((jnp.where(hit, 1.0, 0.0) * inside).astype(jnp.bfloat16))
        begin = begin + amount
    links = jnp.concatenate([window[b] for b in range(blocks)], axis=1)
    upper = links // 16
    lower = links - 16 * upper
    pieces = jnp.concatenate([upper, lower], axis=0).astype(jnp.float32).astype(jnp.bfloat16)
    found = jnp.dot(
        pieces, jnp.concatenate(picks, axis=0), preferred_element_type=jnp.float32
    )
    stations = 16.0 * found[0:2] + found[2:4]
    table = channel_gain[...].reshape(blocks * 4, channel_gain.shape[2])
    high = table.astype(jnp.bfloat16)
    rest = table - high.astype(jnp.float32)
    middle = rest.astype(jnp.bfloat16)
    low = (rest - middle.astype(jnp.float32)).astype(jnp.bfloat16)
    names = lax.broadcasted_iota(jnp.int32, (table.shape[1], 1), 0).astype(jnp.float32)
    for side in range(2):
        pick = jnp.where(names == stations[side : side + 1], 1.0, 0.0).astype(jnp.bfloat16)
        rows = (
            jnp.dot(high, pick, preferred_element_type=jnp.float32)
            + jnp.dot(middle, pick, preferred_element_type=jnp.float32)
            + jnp.dot(low, pick, preferred_element_type=jnp.float32)
        )
        chosen = member[0] * rows[0:4]
        for b in range(1, blocks):
            chosen = chosen + member[b] * rows[4 * b : 4 * b + 4]
        gains_ref[4 * side : 4 * side + 4, :] = chosen
    idents_ref[0:2, :] = stations
    idents_ref[2:3, :] = channel
    idents_ref[3:4, :] = alive
    idents_ref[4:8, :] = jnp.zeros((4, slots), jnp.float32)


def fourier_kernel(
    block_ref,
    links_ref,
    gain_ref,
    p_ref,
    q_ref,
    c_ref,
    s_ref,
    x_ref,
    o_ref,
    gains_ref,
    idents_ref,
    table,
    total,
    window,
    channel_gain,
    window_sem,
    gain_sem,
):
    step = pl.program_id(0)
    copies = fetch_lookups(
        block_ref, links_ref, gain_ref, window, channel_gain, window_sem, gain_sem
    )

    @pl.when(step == 0)
    def _():
        for copy in copies:
            copy.start()

    @pl.when(step == pl.num_programs(0) - 1)
    def _():
        for copy in copies:
            copy.wait()
        use_lookups(block_ref, links_ref, window, channel_gain, gains_ref, idents_ref)

    facets, _, rows, chunk = x_ref.shape
    subgrids = o_ref.shape[0]
    spread = c_ref.shape[0]
    cosine, sine = c_ref[...], s_ref[...]
    for part in range(chunk // spread):
        lead = p_ref[part : part + 1, :]
        other = q_ref[part : part + 1, :]
        table[part * spread : (part + 1) * spread, :] = (lead * cosine + other * sine).astype(
            jnp.bfloat16
        )
    x = x_ref[...].reshape(facets * 2 * rows, chunk)
    product = jnp.dot(x, table[...], preferred_element_type=jnp.float32)

    @pl.when(step == 0)
    def _():
        total[...] = product

    @pl.when(step > 0)
    def _():
        total[...] += product

    @pl.when(step == pl.num_programs(0) - 1)
    def _():
        lane = lax.broadcasted_iota(jnp.int32, (rows, 2 * MC), 1)
        sign = jnp.where(lane < MC, -1.0, 1.0)
        packed = o_ref.shape[3] // (2 * MC)
        for f in range(facets):
            for s in range(subgrids):
                cut = slice(s * 2 * MC, (s + 1) * 2 * MC)
                first = total[2 * f * rows : (2 * f + 1) * rows, cut]
                second = total[(2 * f + 1) * rows : (2 * f + 2) * rows, cut]
                value = first + sign * pltpu.roll(second, MC, 1)
                j = f % packed
                o_ref[s, f // packed, :, j * 2 * MC : (j + 1) * 2 * MC] = value.astype(jnp.bfloat16)


def fourier(x, subgrids, slots, block_table, links, station_gains):
    facets, _, rows, length = x.shape
    width = subgrids * 2 * MC
    spread = FS // MC
    packed = FGRID if facets % FGRID == 0 else 1
    per_step = CHUNK // spread
    blocks = block_table.shape[1]
    span = slots + 128
    in_place = lambda array: pltpu.with_memory_space_constraint(array, pltpu.HBM)
    factors = [in_place(jnp.asarray(t)) for t in fourier_factors(subgrids)]
    out = (subgrids, facets // packed, rows, packed * 2 * MC)
    return pl.pallas_call(
        fourier_kernel,
        out_shape=(
            jax.ShapeDtypeStruct(out, jnp.bfloat16),
            jax.ShapeDtypeStruct((8, slots), jnp.float32),
            jax.ShapeDtypeStruct((8, slots), jnp.float32),
        ),
        grid=(length // CHUNK,),
        in_specs=[
            pl.BlockSpec(memory_space=pltpu.SMEM),
            pl.BlockSpec(memory_space=pltpu.HBM),
            pl.BlockSpec(memory_space=pltpu.HBM),
            pl.BlockSpec((per_step, width), lambda g: (g, 0)),
            pl.BlockSpec((per_step, width), lambda g: (g, 0)),
            pl.BlockSpec((spread, width), lambda g: (0, 0)),
            pl.BlockSpec((spread, width), lambda g: (0, 0)),
            pl.BlockSpec((facets, 2, rows, CHUNK), lambda g: (0, 0, 0, g)),
        ],
        out_specs=(
            pl.BlockSpec(out, lambda g: (0, 0, 0, 0)),
            pl.BlockSpec((8, slots), lambda g: (0, 0)),
            pl.BlockSpec((8, slots), lambda g: (0, 0)),
        ),
        scratch_shapes=[
            pltpu.VMEM((CHUNK, width), jnp.bfloat16),
            pltpu.VMEM((facets * 2 * rows, width), jnp.float32),
            pltpu.VMEM((blocks, 2, span), jnp.int32),
            pltpu.VMEM((blocks, 4, NST), jnp.float32),
            pltpu.SemaphoreType.DMA((blocks,)),
            pltpu.SemaphoreType.DMA((blocks,)),
        ],
        compiler_params=pltpu.CompilerParams(
            dimension_semantics=("arbitrary",), vmem_limit_bytes=48 << 20
        ),
    )(
        block_table,
        in_place(links),
        in_place(station_gains),
        *factors,
        x,
    )


def subgrid_tables():
    angle = unit_angles(SG, SG, SG)
    re = np.cos(angle) / math.sqrt(SG)
    im = np.sin(angle) / math.sqrt(SG)
    blocks = lambda t: t.reshape(SG, FGRID, MC)
    second = np.stack([blocks(re), -blocks(im)], axis=2).reshape(SG, 2 * SG)
    return [t.astype(jnp.bfloat16) for t in (re, im, second)]


def chirp_line():
    offset = np.arange(SG) - SG // 2
    angle = 2.0 * math.pi * w_chirp * (offset * offset) / float(SG * SG)
    return np.cos(angle).astype(np.float32), np.sin(angle).astype(np.float32)


def model_terms(pred, observed, first, second, alive):
    residual, lead, trail = [], [], []
    for p in range(NPOL):
        f1, f2 = p // 2, p % 2
        pred_re, pred_im = pred[p]
        first_re, first_im = first[2 * f1], first[2 * f1 + 1]
        second_re, second_im = second[2 * f2], second[2 * f2 + 1]
        both_re = first_re * second_re + first_im * second_im
        both_im = first_im * second_re - first_re * second_im
        resid_re = alive * (observed[2 * p] - (both_re * pred_re - both_im * pred_im))
        resid_im = alive * (observed[2 * p + 1] - (both_re * pred_im + both_im * pred_re))
        cross_re = second_re * pred_re + second_im * pred_im
        cross_im = second_im * pred_re - second_re * pred_im
        along_re = first_re * pred_re - first_im * pred_im
        along_im = first_re * pred_im + first_im * pred_re
        residual += [resid_re, resid_im]
        lead.append(
            (-(resid_re * cross_re - resid_im * cross_im), -(resid_re * cross_im + resid_im * cross_re))
        )
        trail.append(
            (-(resid_re * along_re + resid_im * along_im), -(resid_re * along_im - resid_im * along_re))
        )
    leading = [lead[2 * f][r] + lead[2 * f + 1][r] for f in range(2) for r in range(2)]
    trailing = [trail[f][r] + trail[f + 2][r] for f in range(2) for r in range(2)]
    return residual, leading, trailing


def nt_dot(left, right, **kw):
    return lax.dot_general(
        left, right, (((1,), (1,)), ((), ())), preferred_element_type=jnp.float32, **kw
    )


def chirped_rows(taper, chirp_ref):
    wide = taper.astype(jnp.float32)
    return jnp.concatenate(
        [
            taper,
            (wide * chirp_ref[0:1, :]).astype(jnp.bfloat16),
            (wide * chirp_ref[1:2, :]).astype(jnp.bfloat16),
        ],
        axis=0,
    )


def predict_kernel(
    sizes,
    contrib_ref,
    lead_ref,
    trail_ref,
    depth_ref,
    observed_ref,
    gains_ref,
    idents_ref,
    table_re_ref,
    table_im_ref,
    second_ref,
    chirp_ref,
    residual_ref,
    grad_ref,
    got,
    lines,
    tapers,
    right,
    left,
    part_out,
    part_in,
    observed_out,
    observed_in,
    record_out,
    record_in,
    got_send,
    got_recv,
    taper_send,
    taper_recv,
    observed_send,
    observed_recv,
    part_send,
    part_recv,
    record_send,
    record_recv,
):
    subgrids, pols, owners = sizes
    z, p, t = lax.axis_index("facet"), lax.axis_index("pol"), lax.axis_index("tm")
    slots = lead_ref.shape[0]
    _, groups, rows, width = contrib_ref.shape
    mesh_id = pl.DeviceIdType.MESH

    def remote(src, dst, send, recv, peer):
        return pltpu.make_async_remote_copy(
            src_ref=src,
            dst_ref=dst,
            send_sem=send,
            recv_sem=recv,
            device_id=peer,
            device_id_type=mesh_id,
        )

    across_total = subgrids * owners
    plane_total = pols * owners
    across = z * owners + t
    plane = p * owners + t

    def across_peer(d):
        other = lax.rem(across + d, across_total)
        return other, (other // owners, p, lax.rem(other, owners))

    def plane_peer(d):
        other = lax.rem(plane + d, plane_total)
        return other, (z, other // owners, lax.rem(other, owners))

    barrier = pltpu.get_barrier_semaphore()
    for d in range(1, across_total):
        pl.semaphore_signal(barrier, inc=1, device_id=across_peer(d)[1], device_id_type=mesh_id)
    for d in range(1, pols):
        q = lax.rem(p + d, pols)
        for o in range(owners):
            pl.semaphore_signal(barrier, inc=1, device_id=(z, q, o), device_id_type=mesh_id)
    pl.semaphore_wait(barrier, across_total - 1 + (pols - 1) * owners)

    quarter = observed_ref.shape[1]
    place = lax.broadcasted_iota(jnp.int32, (2 * NPOL, slots), 1)
    observed_out[...] = jnp.where(
        (place >= p * quarter) & (place < (p + 1) * quarter),
        jnp.concatenate([observed_ref[...]] * pols, axis=1),
        0.0,
    )
    copies = []
    for d in sorted(range(1, subgrids), key=lambda d: -min(d, subgrids - d)):
        other = lax.rem(z + d, subgrids)
        copies.append(
            remote(contrib_ref.at[other], got.at[z], got_send.at[d], got_recv.at[d], (other, p, t))
        )
    partner = lax.rem(t + 1, owners)
    taper_copies = [
        remote(ref, tapers.at[t, k], taper_send.at[k], taper_recv.at[k], (z, p, partner))
        for k, ref in enumerate((trail_ref, lead_ref))
    ]
    observed_copies = []
    for d in range(1, pols):
        q = lax.rem(p + d, pols)
        observed_copies.append(
            remote(
                observed_out, observed_in.at[p], observed_send.at[d], observed_recv.at[d], (z, q, t)
            )
        )
    for copy in copies + taper_copies + observed_copies:
        copy.start()

    table_re = jnp.concatenate([table_re_ref[i, t] for i in range(FGRID)], axis=0)
    table_im = jnp.concatenate([table_im_ref[i, t] for i in range(FGRID)], axis=0)

    turn = jnp.where(
        lax.broadcasted_iota(jnp.int32, (3 * slots, 2 * MC), 1) < MC, -1.0, 1.0
    )

    def prepare(owner, trail, lead):
        trail3 = chirped_rows(trail, chirp_ref)
        a = jnp.dot(trail3, second_ref[...], preferred_element_type=jnp.float32)
        b = jnp.concatenate(
            [
                turn * pltpu.roll(a[:, j * 2 * MC : (j + 1) * 2 * MC], MC, 1)
                for j in range(a.shape[1] // (2 * MC))
            ],
            axis=1,
        )
        n0, n1, n2 = slice(0, slots), slice(slots, 2 * slots), slice(2 * slots, 3 * slots)
        right[owner, 0:slots, :] = a[n0].astype(jnp.bfloat16)
        right[owner, slots : 2 * slots, :] = (a[n1] - b[n2]).astype(jnp.bfloat16)
        right[owner, 2 * slots : 3 * slots, :] = b[n0].astype(jnp.bfloat16)
        right[owner, 3 * slots : 4 * slots, :] = (b[n1] + a[n2]).astype(jnp.bfloat16)
        lead3 = chirped_rows(lead, chirp_ref)
        u = nt_dot(table_re, lead3)
        v = nt_dot(table_im, lead3)
        left[owner, 0] = u[:, n0]
        left[owner, 1] = v[:, n0]
        left[owner, 2] = u[:, n1] - v[:, n2]
        left[owner, 3] = u[:, n2] + v[:, n1]

    prepare(t, trail_ref[...], lead_ref[...])
    got[z] = contrib_ref[z]
    for copy in taper_copies:
        copy.wait()
    prepare(partner, tapers[partner, 0], tapers[partner, 1])
    for copy in copies:
        copy.wait()
    if width == 2 * SG:
        whole = got[...].reshape(subgrids * groups * rows, width)
    else:
        for f in range(subgrids * groups):
            i, j = f // FGRID, f % FGRID
            lines[i * rows : (i + 1) * rows, j * 2 * MC : (j + 1) * 2 * MC] = got[
                f // groups, f % groups
            ]
        whole = lines[...]
    for o in range(owners):
        spread = nt_dot(whole, right[o])
        for w in range(NW):
            g_re = spread[:, w * slots : (w + 1) * slots]
            g_im = spread[:, (NW + w) * slots : (NW + w + 1) * slots]
            l_re, l_im = left[o, 2 * w], left[o, 2 * w + 1]
            part_out[o, 2 * w : 2 * w + 1, :] = jnp.sum(l_re * g_re - l_im * g_im, axis=0, keepdims=True)
            part_out[o, 2 * w + 1 : 2 * w + 2, :] = jnp.sum(
                l_re * g_im + l_im * g_re, axis=0, keepdims=True
            )
        part_out[o, 2 * NW :, :] = jnp.zeros((8 - 2 * NW, slots), jnp.float32)

    part_copies = []
    for d in range(1, plane_total):
        other, peer = plane_peer(d)
        part_copies.append(
            remote(
                part_out.at[lax.rem(other, owners)],
                part_in.at[plane],
                part_send.at[d],
                part_recv.at[d],
                peer,
            )
        )
    for copy in part_copies:
        copy.start()
    part_in[plane] = part_out[t]
    observed_in[p] = observed_out[...]
    for copy in observed_copies:
        copy.wait()
    observed = observed_in[0]
    for q in range(1, pols):
        observed = observed + observed_in[q]
    depth = depth_ref[...].astype(jnp.float32)
    for copy in part_copies:
        copy.wait()

    pred = []
    per_pol = part_in.shape[0] // NPOL
    for q in range(NPOL):
        block = part_in[q * per_pol]
        for o in range(1, per_pol):
            block = block + part_in[q * per_pol + o]
        pred.append(
            tuple(
                sum(depth[w : w + 1] * block[2 * w + c : 2 * w + c + 1] for w in range(NW))
                for c in range(2)
            )
        )
    gains = gains_ref[...]
    idents = idents_ref[...]
    residual, leading, trailing = model_terms(
        pred,
        [observed[k : k + 1] for k in range(2 * NPOL)],
        [gains[k : k + 1] for k in range(4)],
        [gains[4 + k : 5 + k] for k in range(4)],
        idents[3:4],
    )
    for k in range(3):
        record_out[k : k + 1, :] = idents[k : k + 1]
    for k in range(4):
        record_out[3 + k : 4 + k, :] = leading[k]
        record_out[7 + k : 8 + k, :] = trailing[k]
    record_out[11:, :] = jnp.zeros((5, slots), jnp.float32)
    record_copies = []
    for d in range(1, across_total):
        other, peer = across_peer(d)
        record_copies.append(
            remote(record_out, record_in.at[across], record_send.at[d], record_recv.at[d], peer)
        )
    for copy in record_copies:
        copy.start()
    record_in[across] = record_out[...]
    rest = jnp.concatenate(residual, axis=0)
    own_rest = jnp.zeros((2 * NPOL, quarter), jnp.float32)
    for q in range(pols):
        own_rest = jnp.where(p == q, rest[:, q * quarter : (q + 1) * quarter], own_rest)
    residual_ref[...] = own_rest
    for copy in record_copies:
        copy.wait()

    piece = jnp.concatenate([record_in[d] for d in range(across_total)], axis=1)
    own_count = grad_ref.shape[1]
    index = (z * pols + p) * owners + t
    mine = (index * own_count + lax.broadcasted_iota(jnp.int32, (own_count, 1), 0)).astype(
        jnp.float32
    )
    match_first = mine == piece[0:1]
    match_second = mine == piece[1:2]
    weighted = jnp.concatenate(
        [
            jnp.where(match_first, piece[3 + k : 4 + k], 0.0)
            + jnp.where(match_second, piece[7 + k : 8 + k], 0.0)
            for k in range(4)
        ],
        axis=0,
    )
    high = weighted.astype(jnp.bfloat16)
    low = (weighted - high.astype(jnp.float32)).astype(jnp.bfloat16)
    channel_ids = lax.broadcasted_iota(jnp.int32, (NCH, 1), 0).astype(jnp.float32)
    onehot = jnp.where(channel_ids == piece[2:3], 1.0, 0.0).astype(jnp.bfloat16)
    summed = nt_dot(high, onehot) + nt_dot(low, onehot)
    for k in range(4):
        grad_ref[k] = grad_scale * summed[k * own_count : (k + 1) * own_count]


def predict(sizes, own_count, *operands):
    subgrids, pols, owners = sizes
    contrib, lead = operands[0], operands[1]
    _, groups, rows, width = contrib.shape
    slots = lead.shape[0]
    vmem = pl.BlockSpec(memory_space=pltpu.VMEM)
    dma = lambda n: pltpu.SemaphoreType.DMA((n,))
    across_total, plane_total = subgrids * owners, pols * owners
    return pl.pallas_call(
        functools.partial(predict_kernel, sizes),
        out_shape=(
            jax.ShapeDtypeStruct((2 * NPOL, slots // pols), jnp.float32),
            jax.ShapeDtypeStruct((4, own_count, NCH), jnp.float32),
        ),
        in_specs=[vmem] * len(operands),
        out_specs=(vmem, vmem),
        scratch_shapes=[
            pltpu.VMEM(contrib.shape, jnp.bfloat16),
            pltpu.VMEM((FGRID * rows, 2 * SG), jnp.bfloat16),
            pltpu.VMEM((owners, 2, slots, SG), jnp.bfloat16),
            pltpu.VMEM((owners, 2 * NW * slots, 2 * SG), jnp.bfloat16),
            pltpu.VMEM((owners, 4, FGRID * rows, slots), jnp.float32),
            pltpu.VMEM((owners, 8, slots), jnp.float32),
            pltpu.VMEM((plane_total, 8, slots), jnp.float32),
            pltpu.VMEM((8, slots), jnp.float32),
            pltpu.VMEM((pols, 8, slots), jnp.float32),
            pltpu.VMEM((16, slots), jnp.float32),
            pltpu.VMEM((across_total, 16, slots), jnp.float32),
            dma(subgrids),
            dma(subgrids),
            dma(2),
            dma(2),
            dma(pols),
            dma(pols),
            dma(plane_total),
            dma(plane_total),
            dma(across_total),
            dma(across_total),
        ],
        compiler_params=pltpu.CompilerParams(
            collective_id=0, has_side_effects=True, vmem_limit_bytes=48 << 20
        ),
    )(*operands)


def on_device(
    tile_spectral_lines,
    taper_leading_axis,
    taper_trailing_axis,
    depth_layer_factors,
    measured_correlations,
    visibility_groups_table,
    antenna_links,
    complex_receiver_factors,
):
    sizes = tuple(lax.axis_size(name) for name in ("facet", "pol", "tm"))
    subgrids, pols, owners = sizes
    slots = taper_leading_axis.shape[2]
    quarter = measured_correlations.shape[3]
    rows = tile_spectral_lines.shape[3]

    block_table = visibility_groups_table.reshape(3, visibility_groups_table.shape[3])
    observed = measured_correlations.reshape(2 * NPOL, quarter)

    contrib, gains, idents = fourier(
        tile_spectral_lines[:, 0],
        subgrids,
        slots,
        block_table,
        antenna_links,
        complex_receiver_factors,
    )
    table_re, table_im, second = [jnp.asarray(t) for t in subgrid_tables()]
    cosine, sine = chirp_line()
    own_count = NST // (subgrids * pols * owners)
    residual, grad = predict(
        sizes,
        own_count,
        contrib,
        taper_leading_axis.reshape(slots, SG),
        taper_trailing_axis.reshape(slots, SG),
        depth_layer_factors.reshape(NW, slots),
        observed,
        gains,
        idents,
        table_re.reshape(FGRID, owners, rows, SG),
        table_im.reshape(FGRID, owners, rows, SG),
        second,
        jnp.asarray(np.stack([cosine, sine])),
    )
    gain_grad = jnp.transpose(grad, (1, 2, 0)).reshape(own_count, 4 * NCH)
    return residual.reshape(1, 2 * NPOL, 1, quarter), gain_grad


def solution(mesh):
    return jax.shard_map(
        on_device,
        mesh=mesh,
        in_specs=(
            P("facet", "pol", None, "tm", None),
            P("facet", "tm", None, None),
            P("facet", "tm", None, None),
            P("facet", "tm", None, None),
            P("facet", None, "tm", "pol"),
            P("facet", "tm", None, None),
            P(),
            P(),
        ),
        out_specs=(P("facet", None, "tm", "pol"), P(("facet", "pol", "tm"), None)),
        check_vma=False,
    )
```
